512 devices in a mesh: gx: 8 (over z_hi, x), gy: 8 (over y), gz: 8 (over z_lo, core).
Axes of the slice: x: 4, y: 8, z: 8 (z_hi: 2, z_lo: 4; z = z_hi * 4 + z_lo), core: 2. Of those that a mesh axis runs over, the one named last changes fastest.
Arguments:
- features: float32 [2048, 64, 512], P(('gx', 'gy', 'gz')), may hold values from -6 to 6
- preact: float32 [2048, 64, 512], P(('gx', 'gy', 'gz')), may hold values from -10 to 10
- cotangent: float32 [2048, 64, 512], P(('gx', 'gy', 'gz')), may hold values from -6 to 6
- kernel: float32 [27, 64, 64], replicated, may hold values from -0.15625 to 0.15625
- active: int32 [2048, 512], P(('gx', 'gy', 'gz')), may hold values from 0 to 1, as said below
- owner_dir: int32 [2048, 27], P(('gx', 'gy', 'gz')), may hold values from 0 to 27, as said below
- owner_slot: int32 [2048, 27], P(('gx', 'gy', 'gz')), may hold values from 0 to 3, as said below
- send_list: int32 [1536], P(('gx', 'gy', 'gz')), may hold values from 0 to 4, as said below
Outputs:
- input_grad: float32 [2048, 64, 512], P(('gx', 'gy', 'gz'))
- kernel_grad: float32 [27, 64, 64], replicated
- bias_grad: float32 [64], replicated
The draws below stay inside these ranges and needn't reach their ends.
Inputs may be any that keep to these rules, and one draw needn't show every extreme that they name: `owner_dir`: 27 where the neighbouring block is empty or the stored entry is unused; 13 for a block of the same partition; else the offset of the owner's grid position, 9 (dx + 1) + 3 (dy + 1) + (dz + 1), with dx, dy, dz each -1, 0 or 1. A named partition always exists and lists the block in its send list. `owner_slot`: own stored index where owner_dir is 13, position in the owner's send list where owner_dir names another partition, 0 where it is 27. `send_list`: each partition's 3 entries hold, increasing, the distinct stored indices of its occupied blocks in the partition's outer layer of blocks (on faces, edges or corners), each of which touches another partition, then 4 for unused entries; some partition fills all 3. 1 for active voxels of an occupied stored block, 0 elsewhere; unused stored entries are 0 throughout; some partition has all 4 entries occupied.
All inputs are finite; a program needn't handle non-finite values.
Results may differ from the reference program's by a relative error of at most 0.0001.
Values sent between devices are 32-bit elements; how exact they have to be, the bound alone decides.
No kernel may reach another device: no remote copies, remote signals or barrier semaphores. Data moves between devices by JAX's collectives and lax.ppermute only.
A program may use at most 64 MiB of HBM per device.

```python
import jax
import jax.numpy as jnp
from jax import lax

C = 64
BS = 8
PB = 6
SEND = 3
BLK_DEV = 4
VOL = 512
NB_ALL = 2048
N_GX = 8
N_GY = 8
N_GZ = 8


def block_layout(key):
    subkeys = jax.random.split(jax.random.fold_in(key, 7), 12)
    size_x, size_y, size_z = (N_GX, N_GY, N_GZ)
    devices = size_x * size_y * size_z
    part_side = PB
    slot_count = part_side ** 3
    inner_side = part_side - 2
    device_ids = jnp.arange(devices, dtype=jnp.int32)
    coord_x = device_ids // (size_y * size_z)
    coord_y = device_ids // size_z % size_y
    coord_z = device_ids % size_z
    slot_ids = jnp.arange(slot_count, dtype=jnp.int32)
    local_x = slot_ids // (part_side * part_side)
    local_y = slot_ids // part_side % part_side
    local_z = slot_ids % part_side
    forced_x = jax.random.randint(subkeys[0], (), 0, size_x - 1)
    forced_y = jax.random.randint(subkeys[1], (), 0, size_y - 1)
    forced_z = jax.random.randint(subkeys[2], (), 0, size_z - 1)
    parity_flag = (forced_x + forced_y + forced_z) % 2
    creator = (coord_x + coord_y + coord_z) % 2 == parity_flag
    forced = (forced_x * size_y + forced_y) * size_z + forced_z
    is_forced = device_ids == forced
    link_draw = jax.random.randint(subkeys[3], (devices, 3), 0, 10) < 6
    has_next = jnp.stack([coord_x < size_x - 1, coord_y < size_y - 1, coord_z < size_z - 1], axis=1)
    link_on = creator[:, None] & has_next & (link_draw | is_forced[:, None])
    spot_first = jax.random.randint(subkeys[4], (devices, 3), 0, part_side)
    spot_second = jax.random.randint(subkeys[5], (devices, 3), 0, part_side)
    inner_first = jax.random.randint(subkeys[6], (devices, 3), 1, part_side - 1)
    inner_second = jax.random.randint(subkeys[7], (devices, 3), 1, part_side - 1)
    spot_first = jnp.where(is_forced[:, None], inner_first, spot_first)
    spot_second = jnp.where(is_forced[:, None], inner_second, spot_second)
    rim_count = jnp.zeros((devices, slot_count), jnp.int32)
    strides = [size_y * size_z, size_z, 1]
    for axis_index in range(3):
        first = spot_first[:, axis_index]
        second = spot_second[:, axis_index]
        link_value = link_on[:, axis_index].astype(jnp.int32)
        if axis_index == 0:
            source_slot = ((part_side - 1) * part_side + first) * part_side + second
            target_slot = first * part_side + second
        elif axis_index == 1:
            source_slot = (first * part_side + part_side - 1) * part_side + second
            target_slot = first * part_side * part_side + second
        else:
            source_slot = (first * part_side + second) * part_side + part_side - 1
            target_slot = (first * part_side + second) * part_side
        target_dev = jnp.where(link_value > 0, device_ids + strides[axis_index], device_ids)
        rim_count = rim_count.at[device_ids, source_slot].max(link_value)
        rim_count = rim_count.at[target_dev, target_slot].max(link_value)
    rim_live = rim_count > 0
    inner_slot = (local_x >= 1) & (local_x <= part_side - 2) & (local_y >= 1) & (local_y <= part_side - 2) & (local_z >= 1) & (local_z <= part_side - 2)
    rim_slot = jnp.logical_not(inner_slot)
    inner_index = jnp.where(inner_slot, ((local_x - 1) * inner_side + (local_y - 1)) * inner_side + (local_z - 1), 0)
    capacity = BLK_DEV - SEND
    heavy_part = jax.random.randint(subkeys[8], (devices,), 0, 4) == 0
    light_count = jax.random.randint(subkeys[9], (devices,), 0, 2)
    counts = jnp.where(heavy_part | is_forced, capacity, light_count)
    inner_total = inner_side ** 3
    scores = jax.random.randint(subkeys[10], (devices, inner_total), 0, 2 ** 20) * inner_total + jnp.arange(inner_total, dtype=jnp.int32)[None, :]
    ranking = jnp.argsort(jnp.argsort(scores, axis=1), axis=1).astype(jnp.int32)
    inner_live = inner_slot[None, :] & (ranking[:, inner_index] < counts[:, None])
    occupied = rim_live | inner_live
    priority = jax.random.randint(subkeys[11], (devices, slot_count), 0, 2 ** 20) * slot_count + slot_ids[None, :]
    priority = jnp.where(occupied, priority, priority + 2 ** 30)
    stored_slot = jnp.argsort(priority, axis=1)[:, :BLK_DEV].astype(jnp.int32)
    stored_live = jnp.take_along_axis(occupied, stored_slot, axis=1)
    store_ids = jnp.arange(BLK_DEV, dtype=jnp.int32)
    slot_store = jnp.zeros((devices, slot_count), jnp.int32).at[device_ids[:, None], stored_slot].set(jnp.broadcast_to(store_ids[None, :], (devices, BLK_DEV)))
    stored_rim = rim_slot[stored_slot] & stored_live
    position = jnp.cumsum(stored_rim.astype(jnp.int32), axis=1) - 1
    send_rows = []
    for position_index in range(SEND):
        matched = stored_rim & (position == position_index)
        found_index = jnp.sum(jnp.where(matched, store_ids[None, :], 0), axis=1) + jnp.where(jnp.any(matched, axis=1), 0, BLK_DEV)
        send_rows.append(found_index)
    send_table = jnp.stack(send_rows, axis=1).astype(jnp.int32)
    store_position = jnp.where(stored_rim, position, 0)
    offsets = jnp.arange(27, dtype=jnp.int32)
    shift_x = offsets // 9 - 1
    shift_y = offsets // 3 % 3 - 1
    shift_z = offsets % 3 - 1
    global_x = coord_x[:, None, None] * part_side + local_x[stored_slot][:, :, None] + shift_x[None, None, :]
    global_y = coord_y[:, None, None] * part_side + local_y[stored_slot][:, :, None] + shift_y[None, None, :]
    global_z = coord_z[:, None, None] * part_side + local_z[stored_slot][:, :, None] + shift_z[None, None, :]
    inside = (global_x >= 0) & (global_x < size_x * part_side) & (global_y >= 0) & (global_y < size_y * part_side) & (global_z >= 0) & (global_z < size_z * part_side)
    global_x = jnp.clip(global_x, 0, size_x * part_side - 1)
    global_y = jnp.clip(global_y, 0, size_y * part_side - 1)
    global_z = jnp.clip(global_z, 0, size_z * part_side - 1)
    owner_x = global_x // part_side
    owner_y = global_y // part_side
    owner_z = global_z // part_side
    owner_dev = (owner_x * size_y + owner_y) * size_z + owner_z
    near_slot = (global_x % part_side * part_side + global_y % part_side) * part_side + global_z % part_side
    near_live = occupied[owner_dev, near_slot] & inside & stored_live[:, :, None]
    direction = (owner_x - coord_x[:, None, None] + 1) * 9 + (owner_y - coord_y[:, None, None] + 1) * 3 + (owner_z - coord_z[:, None, None] + 1)
    own_store = slot_store[owner_dev, near_slot]
    remote = store_position[owner_dev, own_store]
    dir_table = jnp.where(near_live, direction, 27).astype(jnp.int32)
    slot_table = jnp.where(near_live, jnp.where(direction == 13, own_store, remote), 0).astype(jnp.int32)
    return (stored_live, dir_table.reshape(devices * BLK_DEV, 27), slot_table.reshape(devices * BLK_DEV, 27), send_table.reshape(devices * SEND))


def draw_active(key, part):
    stored_live = block_layout(key)[0]
    devices = N_GX * N_GY * N_GZ
    flips = jax.random.randint(jax.random.fold_in(key, 11), (devices * BLK_DEV, BS ** 3), 0, 10) < 6
    return (flips & stored_live.reshape(devices * BLK_DEV)[:, None]).astype(jnp.int32)


def draw_owner_dir(key, part):
    return block_layout(key)[1]


def draw_owner_slot(key, part):
    return block_layout(key)[2]


def draw_send_list(key, part):
    return block_layout(key)[3]


def block_scale(key, shape, shards, smallest, top_value):
    def one(axis_at, parts):
        heights = jax.random.uniform(jax.random.fold_in(jax.random.fold_in(key, 6), axis_at), (parts,), jnp.float32, smallest / len(shards), top_value / len(shards))
        return jnp.repeat(jnp.exp(heights), shape[axis_at] // parts).reshape((-1,) + (1,) * (len(shape) - axis_at - 1))

    loudness = one(*shards[0])
    for cut in shards[1:]:
        loudness = loudness * one(*cut)
    return loudness


def noise(key, dims, spread, bound, cuts=(), kind=jnp.bfloat16):
    drawn = jax.random.normal(key, dims, jnp.float32) * spread
    if len(cuts) > 0:
        drawn = block_scale(key, dims, cuts, -0.22, 0.18) * drawn
    return jnp.clip(drawn, min=-bound, max=bound).astype(kind)


def setup_inputs(seed: int = 0) -> dict:
    streams_of = jax.random.split(jax.random.key(seed), 9)
    features = noise(streams_of[0], (NB_ALL, C, VOL), 1.0, 6.0, ((0, 512),), jnp.float32)
    preact = noise(streams_of[1], (NB_ALL, C, VOL), 2.0, 10.0, ((0, 512),), jnp.float32)
    cotangent = noise(streams_of[2], (NB_ALL, C, VOL), 1.0, 6.0, ((0, 512),), jnp.float32)
    kernel = noise(streams_of[3], (27, C, C), (27 * C) ** -0.5, 0.15625, (), jnp.float32)
    active = draw_active(jax.random.fold_in(streams_of[8], 71), 0)
    owner_dir = draw_owner_dir(jax.random.fold_in(streams_of[8], 71), 0)
    owner_slot = draw_owner_slot(jax.random.fold_in(streams_of[8], 71), 0)
    send_list = draw_send_list(jax.random.fold_in(streams_of[8], 71), 0)
    return dict(features=features, preact=preact, cotangent=cotangent, kernel=kernel, active=active, owner_dir=owner_dir, owner_slot=owner_slot, send_list=send_list)


def silu_slope(preact):
    sigmoid_value = jax.nn.sigmoid(preact)
    return sigmoid_value * (1.0 + preact * (1.0 - sigmoid_value))


def neighbourhood(source, targets, extent):
    anchor = jnp.zeros((), jnp.int32)
    channels = source.shape[1]
    layers = []
    for place_x in range(3):
        strips = []
        for place_y in range(3):
            pieces = []
            for place_z in range(3):
                places = (place_x, place_y, place_z)
                begins = [anchor + (extent - 1 if where_at == 0 else 0) for where_at in places]
                lengths = [extent if where_at == 1 else 1 for where_at in places]
                chosen = targets[place_x * 9 + place_y * 3 + place_z].astype(jnp.int32)
                portion = lax.dynamic_slice(source, [chosen, anchor] + begins, [1, channels] + lengths)
                pieces.append(portion[0])
            strips.append(jnp.concatenate(pieces, axis=3))
        layers.append(jnp.concatenate(strips, axis=2))
    return jnp.concatenate(layers, axis=1)


def shifted_stack(padded, direction, extent):
    windows = []
    for offset_x in (-1, 0, 1):
        for offset_y in (-1, 0, 1):
            for offset_z in (-1, 0, 1):
                begin_x = 1 + direction * offset_x
                begin_y = 1 + direction * offset_y
                begin_z = 1 + direction * offset_z
                window = padded[:, begin_x:begin_x + extent, begin_y:begin_y + extent, begin_z:begin_z + extent]
                windows.append(window.reshape(padded.shape[0], extent ** 3))
    return jnp.stack(windows)


def reference(features, preact, cotangent, kernel, active, owner_dir, owner_slot, send_list):
    blocks_all, channels, volume = features.shape
    extent = BS
    devices = N_GX * N_GY * N_GZ
    block_ids = jnp.arange(blocks_all, dtype=jnp.int32)
    device_ids = block_ids // BLK_DEV
    coord_x = device_ids // (N_GY * N_GZ)
    coord_y = (device_ids // N_GZ) % N_GY
    coord_z = device_ids % N_GZ
    step_x = owner_dir // 9 - 1
    step_y = (owner_dir // 3) % 3 - 1
    step_z = owner_dir % 3 - 1
    owner_dev = ((coord_x[:, None] + step_x) * N_GY + coord_y[:, None] + step_y) * N_GZ + coord_z[:, None] + step_z
    owner_dev = jnp.clip(owner_dev, 0, devices - 1).astype(jnp.int32)
    listed = send_list[jnp.clip(owner_dev * SEND + owner_slot, 0, devices * SEND - 1)]
    remote_index = owner_dev * BLK_DEV + jnp.clip(listed, 0, BLK_DEV - 1)
    local_index = device_ids[:, None] * BLK_DEV + owner_slot
    source_index = jnp.where(owner_dir == 13, local_index, remote_index)
    source_index = jnp.where(owner_dir < 27, source_index, 0).astype(jnp.int32)
    valid_mask = (owner_dir < 27).astype(jnp.float32)
    every_place = jnp.arange(27, dtype=jnp.int32)

    def visit_block(running, inputs):
        kernel_partial, bias_partial = running
        indices, weights, block_index = inputs
        near_mask = active[indices].astype(jnp.float32)[:, None, :] * weights[:, None, None]
        near_grad = cotangent[indices] * silu_slope(preact[indices]) * near_mask
        near_input = features[indices] * near_mask
        cube_shape = (27, channels, extent, extent, extent)
        grad_windows = shifted_stack(neighbourhood(near_grad.reshape(cube_shape), every_place, extent), -1, extent)
        input_windows = shifted_stack(neighbourhood(near_input.reshape(cube_shape), every_place, extent), 1, extent)
        block_mask = active[block_index].astype(jnp.float32)[None, :]
        own_grad = cotangent[block_index] * silu_slope(preact[block_index]) * block_mask
        block_result = jnp.einsum("kio,kov->iv", kernel, grad_windows, precision=lax.Precision.HIGHEST) * block_mask
        kernel_partial = kernel_partial + jnp.einsum("kiv,ov->kio", input_windows, own_grad, precision=lax.Precision.HIGHEST)
        bias_partial = bias_partial + jnp.sum(own_grad, axis=1)
        return (kernel_partial, bias_partial), block_result

    initial = (jnp.zeros((27, channels, channels), jnp.float32), jnp.zeros((channels,), jnp.float32))
    (kernel_partial, bias_partial), input_grad = lax.scan(visit_block, initial, (source_index, valid_mask, block_ids))
    scaling = (volume * blocks_all) ** -0.5
    return input_grad, kernel_partial * scaling, bias_partial * scaling
```

```python
import functools

import jax
import jax.numpy as jnp
import numpy as np
from jax import lax
from jax.experimental import pallas as pl
from jax.experimental.pallas import tpu as pltpu
from jax.sharding import Mesh, PartitionSpec as P

F32 = jnp.float32
BF16 = jnp.bfloat16
BS = 8
VOL = 512
LANES = 128
PAY = 1024
AX = ("gx", "gy", "zl", "core")
AXZ = ("zl", "core")

FACE = 64


def layout_of(blocks, listed):
    own = blocks * VOL
    face = listed * FACE
    edge = listed * BS
    corner = -(-listed // 8) * 8
    y_rows = face + 2 * edge
    z_rows = face + 4 * edge + 4 * corner
    starts = [own]
    for size in (face, face, y_rows, y_rows, z_rows):
        starts.append(starts[-1] + size)
    total = starts[-1] + z_rows
    return dict(face=face, edge=edge, corner=corner, y_rows=y_rows, z_rows=z_rows,
                starts=starts, total=total)


def log2(n):
    return int(n).bit_length() - 1


def piece_table(blocks, listed):
    lay = layout_of(blocks, listed)
    face, edge, corner, starts = lay["face"], lay["edge"], lay["corner"], lay["starts"]
    table = np.zeros((27, 28), np.int32)
    for o in range(27):
        off = (o // 9 - 1, o // 3 % 3 - 1, o % 3 - 1)
        if off == (0, 0, 0):
            continue
        fixed = [7 if v == -1 else 0 for v in off]
        axis = 0 if off[0] else (1 if off[1] else 2)
        plane = [i for i in range(3) if i != axis]
        for d in range(27):
            own = (d // 9 - 1, d // 3 % 3 - 1, d % 3 - 1)
            if any(v != 0 and v != w for v, w in zip(own, off)):
                continue
            side = [(v + 1) // 2 for v in own]
            if own == (0, 0, 0):
                base, mult, strides = 0, VOL, {0: 64, 1: 8, 2: 1}
            elif own[2]:
                base = starts[4 + side[2]]
                if own[0] and own[1]:
                    base += face + 4 * edge + corner * (side[1] * 2 + side[0])
                    mult, strides = 1, {}
                elif own[0]:
                    base += face + edge * side[0]
                    mult, strides = 8, {1: 1}
                elif own[1]:
                    base += face + 2 * edge + edge * side[1]
                    mult, strides = 8, {0: 1}
                else:
                    mult, strides = 64, {0: 8, 1: 1}
            elif own[1]:
                base = starts[2 + side[1]]
                if own[0]:
                    base += face + edge * side[0]
                    mult, strides = 8, {2: 1}
                else:
                    mult, strides = 64, {0: 8, 2: 1}
            else:
                base = starts[side[0]]
                mult, strides = 64, {1: 8, 2: 1}
            for i in range(3):
                if off[i] != 0:
                    base += fixed[i] * strides.get(i, 0)
            s1 = strides[plane[0]] if off[plane[0]] == 0 else 1
            s2 = strides[plane[1]] if off[plane[1]] == 0 else 1
            table[o, d] = base | log2(mult) << 12 | log2(s1) << 16 | log2(s2) << 20
    return table.reshape(-1)


def split_hl(value, mask):
    high = value.astype(BF16).astype(F32)
    return jnp.where(mask, high, value - high)


def prep_kernel(send, cot, pre, act, gd, xs, ys, zs):
    blocks = cot.shape[0]
    listed = send.shape[0]
    for b in range(blocks):
        p = pre[b]
        s = 1.0 / (1.0 + jnp.exp(-p))
        m = act[b : b + 1, :].astype(F32)
        g = cot[b] * (s * (1.0 + p * (1.0 - s))) * m
        gd[b * VOL : (b + 1) * VOL, :] = jnp.concatenate([g, g], axis=0).T
    for i in range(listed):
        r0 = pl.multiple_of(jnp.minimum(send[i], blocks - 1) * VOL, VOL)
        for side in range(2):
            f = 7 * side
            xs[side, i * 64 : (i + 1) * 64, :] = gd[pl.ds(r0 + f * 64, 64), :]
            for x in range(8):
                ys[side, i * 64 + x * 8 : i * 64 + x * 8 + 8, :] = gd[pl.ds(r0 + x * 64 + f * 8, 8), :]
            zs[side, i * 64 : (i + 1) * 64, :] = gd[pl.ds(r0 + f, 64, stride=8), :]


def pack_y_kernel(ys, rx0, rx1, out0, out1):
    face = ys.shape[1]
    listed = face // 64
    for side, out in ((0, out0), (1, out1)):
        f = 7 * side
        out[0:face, :] = ys[side]
        for j, rx in enumerate((rx0, rx1)):
            for s in range(listed):
                row = face + (j * listed + s) * 8
                out[row : row + 8, :] = rx[s * 64 + f * 8 : s * 64 + f * 8 + 8, :]


def pack_z_kernel(zs, rx0, rx1, ry0, ry1, out0, out1):
    face = zs.shape[1]
    listed = face // 64
    edge = listed * 8
    corner = -(-listed // 8) * 8
    for side, out in ((0, out0), (1, out1)):
        f = 7 * side
        out[0:face, :] = zs[side]
        for j, src in enumerate((rx0, rx1, ry0, ry1)):
            row = face + j * edge
            out[row : row + edge, :] = src[pl.ds(f, edge, stride=8), :]
        for j, src in enumerate((ry0, ry1)):
            for i in range(2):
                row = face + 4 * edge + corner * (2 * j + i)
                out[row : row + corner, :] = jnp.zeros((corner, LANES), F32)
                for s in range(listed):
                    at = face + i * edge + s * 8 + f
                    out[row + s : row + s + 1, :] = src[at : at + 1, :]


def main_kernel(gd, feat, act, kern, at, p, kg, rt, bias, z):
    b = pl.program_id(0)
    lane = lax.broadcasted_iota(jnp.int32, (VOL, LANES), 1) < 64

    @pl.when(b == 0)
    def _():
        kg[...] = jnp.zeros(kg.shape, F32)
        bias[...] = jnp.zeros(bias.shape, F32)
        for k in range(27):
            kx, c = k // 9, k % 9
            w = kern[k]
            wd = jnp.concatenate([w, w], axis=1)
            high = wd.astype(BF16)
            low = (wd - high.astype(F32)).astype(BF16)
            rt[kx * 128 : kx * 128 + 64, c * 128 : (c + 1) * 128] = high
            rt[kx * 128 + 64 : kx * 128 + 128, c * 128 : (c + 1) * 128] = low

    g = gd[...]
    bias[0:1, :] += jnp.sum(g, axis=0, keepdims=True)
    hl = split_hl(g, lane)
    row = lax.broadcasted_iota(jnp.int32, (VOL, LANES), 0)
    vy = (row // 8) % 8
    vz = row % 8
    for kz in (-1, 0, 1):
        if kz == 0:
            sz = hl
        elif kz == 1:
            sz = jnp.where(vz >= 1, pltpu.roll(hl, 1, 0), 0.0)
        else:
            sz = jnp.where(vz <= 6, pltpu.roll(hl, VOL - 1, 0), 0.0)
        for ky in (-1, 0, 1):
            if ky == 0:
                sy = sz
            elif ky == 1:
                sy = jnp.where(vy >= 1, pltpu.roll(sz, 8, 0), 0.0)
            else:
                sy = jnp.where(vy <= 6, pltpu.roll(sz, VOL - 8, 0), 0.0)
            c = (ky + 1) * 3 + kz + 1
            z[:, c * 128 : (c + 1) * 128] = sy.astype(BF16)

    f = feat[0] * act[pl.ds(b, 1), :].astype(F32)
    ff = jnp.concatenate([f, f], axis=0)
    half = lax.broadcasted_iota(jnp.int32, (LANES, VOL), 0) < 64
    a = split_hl(ff, half)
    at[...] = a.T
    zero = jnp.zeros((LANES, 64), F32)
    up = jnp.concatenate([zero, a[:, : VOL - 64]], axis=1)
    down = jnp.concatenate([a[:, 64:], zero], axis=1)
    a3 = jnp.concatenate([up, a, down], axis=0).astype(BF16)
    kg[...] += jnp.dot(a3, z[...], preferred_element_type=F32)
    p3 = lax.dot_general(z[...], rt[...], (((1,), (1,)), ((), ())), preferred_element_type=F32)
    p[...] = p3[:, 128:256]
    p[64:VOL, :] += p3[: VOL - 64, 256:384]
    p[0 : VOL - 64, :] += p3[64:, 0:128]


def nt(a, b):
    return lax.dot_general(a, b, (((1,), (1,)), ((), ())), preferred_element_type=F32)


def tn(a, b):
    return lax.dot_general(a, b, (((0,), (0,)), ((), ())), preferred_element_type=F32)


def plane_pieces(axis, sign):
    out = []
    for o in range(27):
        off = (o // 9 - 1, o // 3 % 3 - 1, o % 3 - 1)
        if off[axis] == sign and all(off[i] == 0 for i in range(axis)):
            r, q = [off[i] for i in range(3) if i != axis]
            out.append((o, r, q))
    return out


def halo_kernel(scale, od, os_, tb, core, gd, rx0, rx1, ry0, ry1, rz0, rz1, at, rt, kgm, bias, p, act,
                mine, other, ig, src, pb, pw, kg, pa, pay):
    blocks = od.shape[0]
    row = 0
    for ref in (gd, rx0, rx1, ry0, ry1, rz0, rz1):
        src[row : row + ref.shape[0], :] = ref[...]
        row += ref.shape[0]
    kg[...] = kgm[...]
    pa[...] = p[...]
    lane64 = lax.broadcasted_iota(jnp.int32, (64, LANES), 1) < 64

    def plane(b, axis, sign):
        face = 0 if sign == -1 else 7
        pb[...] = jnp.zeros(pb.shape, F32)
        for o, r, q in plane_pieces(axis, sign):
            d = od[b, o]

            @pl.when(d != 27)
            def _(o=o, r=r, q=q, d=d):
                code = tb[o * 28 + d]
                base = (code & 4095) + (os_[b, o] << ((code >> 12) & 15))
                sr = (code >> 16) & 15
                sq = (code >> 20) & 15
                for i in range(8 if r == 0 else 1):
                    for j in range(8 if q == 0 else 1):
                        at_r = i + 1 if r == 0 else (0 if r == -1 else 9)
                        at_q = 8 + j if q == 0 else (7 if q == -1 else 16)
                        row = base + (i << sr) + (j << sq)
                        pb[at_r, at_q : at_q + 1, :] = src[pl.ds(row, 1), :]

        for kr in (-1, 0, 1):
            for kq in (-1, 0, 1):
                win = pb[1 - kr : 9 - kr, 8 - kq : 16 - kq, :].reshape(64, LANES)
                c = (kr + 1) * 3 + kq + 1
                pw[:, c * 128 : (c + 1) * 128] = split_hl(win, lane64).astype(BF16)
        r0 = b * VOL
        k = 1 - sign
        if axis == 0:
            rows = pl.ds(pl.multiple_of(r0 + face * 64, 64), 64)
            ap = at[rows, :].astype(BF16)
            span = slice(k * 128, (k + 1) * 128)
            kg[span, :] += tn(ap, pw[...])
            pa[rows, :] += nt(pw[...], rt[span, :])
        elif axis == 1:
            starts = [pl.multiple_of(r0 + x * 64 + face * 8, 8) for x in range(8)]
            ap = jnp.concatenate([at[pl.ds(s, 8), :] for s in starts], axis=0).astype(BF16)
            acc = jnp.zeros((64, LANES), F32)
            cols = slice(k * 384, (k + 1) * 384)
            for i in range(3):
                part = pw[:, i * 384 : (i + 1) * 384]
                kg[i * 128 : (i + 1) * 128, cols] += tn(ap, part)
                acc = acc + nt(part, rt[i * 128 : (i + 1) * 128, cols])
            for x, s in enumerate(starts):
                pa[pl.ds(s, 8), :] += acc[x * 8 : x * 8 + 8, :]
        else:
            rows = pl.ds(r0 + face, 64, stride=8)
            ap = at[rows, :].astype(BF16)
            acc = jnp.zeros((64, LANES), F32)
            for i in range(3):
                for j in range(3):
                    part = pw[:, (i * 3 + j) * 128 : (i * 3 + j + 1) * 128]
                    cols = slice((j * 3 + k) * 128, (j * 3 + k + 1) * 128)
                    kg[i * 128 : (i + 1) * 128, cols] += tn(ap, part)
                    acc = acc + nt(part, rt[i * 128 : (i + 1) * 128, cols])
            pa[rows, :] = pa[rows, :] + acc

    def block(b, carry):
        for axis in range(3):
            for sign in (-1, 1):
                found = od[b, plane_pieces(axis, sign)[0][0]] != 27
                for o, _, _ in plane_pieces(axis, sign)[1:]:
                    found = found | (od[b, o] != 27)

                @pl.when(found)
                def _(axis=axis, sign=sign):
                    plane(b, axis, sign)

        return carry

    lax.fori_loop(0, blocks, block, 0)

    for n in range(28):
        t, odd = n // 2, n % 2
        if n < 27:
            kx, c = n // 9, n % 9
            lo, hi = c * 128, (c + 1) * 128
            u = kg[kx * 128 : kx * 128 + 64, lo:hi] + kg[kx * 128 + 64 : kx * 128 + 128, lo:hi]
            u = u + pltpu.roll(u, 64, 1)
        else:
            first = lax.broadcasted_iota(jnp.int32, (64, LANES), 0) == 0
            u = jnp.where(first, jnp.broadcast_to(bias[0:1, :], (64, LANES)), 0.0)
        if odd:
            pay[t * 64 : (t + 1) * 64, :] = jnp.where(lane64, held, u) * scale
        held = u
    pay[14 * 64 :, :] = jnp.zeros((PAY - 14 * 64, LANES), F32)
    me = core[0]
    mine[...] = pay[pl.ds(pl.multiple_of(me * (PAY // 2), PAY // 2), PAY // 2), :]
    other[...] = pay[pl.ds(pl.multiple_of((1 - me) * (PAY // 2), PAY // 2), PAY // 2), :]
    for b in range(blocks):
        og = pa[b * VOL : (b + 1) * VOL, :]
        og = (og + pltpu.roll(og, 64, 1)).T
        ig[b] = og[:64, :] * act[b : b + 1, :].astype(F32)


def unpack_kernel(core, mine, other, kout, bout, pay):
    me = core[0]
    pay[pl.ds(pl.multiple_of(me * (PAY // 2), PAY // 2), PAY // 2), :] = mine[...]
    pay[pl.ds(pl.multiple_of((1 - me) * (PAY // 2), PAY // 2), PAY // 2), :] = other[...]
    for t in range(14):
        tile = pay[t * 64 : (t + 1) * 64, :]
        turned = pltpu.roll(tile, 64, 1)
        kout[2 * t] = tile[:, :64]
        if t < 13:
            kout[2 * t + 1] = turned[:, :64]
        else:
            bout[...] = turned[0:1, :64]


VM = pl.BlockSpec(memory_space=pltpu.VMEM)
SM = pl.BlockSpec(memory_space=pltpu.SMEM)


def sds(shape, dtype=F32):
    return jax.ShapeDtypeStruct(shape, dtype)


def both_ways(low, high, axis):
    n = lax.axis_size(axis)
    up = lax.ppermute(high, axis, [(i, i + 1) for i in range(n - 1)])
    down = lax.ppermute(low, axis, [(i + 1, i) for i in range(n - 1)])
    return up, down


def shards(features, preact, cotangent, kernel, active, owner_dir, owner_slot, send_list):
    blocks, channels, volume = features.shape
    listed = send_list.shape[0]
    lay = layout_of(blocks, listed)
    face, yr, zr = lay["face"], lay["y_rows"], lay["z_rows"]
    devices = lax.axis_size(AX)
    me = lax.axis_index("core").astype(jnp.int32)
    core = me.reshape(1)
    scale = float((volume * blocks * devices) ** -0.5)

    gd, xs, ys, zs = pl.pallas_call(
        prep_kernel,
        out_shape=(sds((blocks * VOL, LANES)),) + (sds((2, face, LANES)),) * 3,
        in_specs=[SM, VM, VM, VM],
        out_specs=(VM,) * 4,
        name="prep",
    )(send_list, cotangent, preact, active)

    rx0, rx1 = both_ways(xs[0], xs[1], "gx")

    full = lambda shape: pl.BlockSpec(shape, lambda b: (0,) * len(shape))
    at, p, kgm, rt, bias = pl.pallas_call(
        main_kernel,
        grid=(blocks,),
        in_specs=[
            pl.BlockSpec((VOL, LANES), lambda b: (b, 0)),
            pl.BlockSpec((1, channels, VOL), lambda b: (b, 0, 0)),
            full((blocks, VOL)),
            full((27, channels, channels)),
        ],
        out_specs=(
            pl.BlockSpec((VOL, LANES), lambda b: (b, 0)),
            pl.BlockSpec((VOL, LANES), lambda b: (b, 0)),
            full((384, 1152)),
            full((384, 1152)),
            full((8, LANES)),
        ),
        out_shape=(
            sds((blocks * VOL, LANES)),
            sds((blocks * VOL, LANES)),
            sds((384, 1152)),
            sds((384, 1152), BF16),
            sds((8, LANES)),
        ),
        scratch_shapes=[pltpu.VMEM((VOL, 1152), BF16)],
        name="interior",
    )(gd, features, active, kernel)

    ys0, ys1 = pl.pallas_call(
        pack_y_kernel, out_shape=(sds((yr, LANES)),) * 2, in_specs=[VM] * 3, out_specs=(VM,) * 2,
        name="pack_y",
    )(ys, rx0, rx1)
    ry0, ry1 = both_ways(ys0, ys1, "gy")
    zs0, zs1 = pl.pallas_call(
        pack_z_kernel, out_shape=(sds((zr, LANES)),) * 2, in_specs=[VM] * 5, out_specs=(VM,) * 2,
        name="pack_z",
    )(zs, rx0, rx1, ry0, ry1)
    rz0, rz1 = both_ways(zs0, zs1, AXZ)

    table = jnp.asarray(piece_table(blocks, listed))
    mine, other, input_grad = pl.pallas_call(
        functools.partial(halo_kernel, scale),
        out_shape=(sds((PAY // 2, LANES)), sds((PAY // 2, LANES)), sds((blocks, channels, VOL))),
        in_specs=[SM] * 4 + [VM] * 13,
        out_specs=(VM,) * 3,
        scratch_shapes=[
            pltpu.VMEM((lay["total"], LANES), F32),
            pltpu.VMEM((10, 24, LANES), F32),
            pltpu.VMEM((64, 1152), BF16),
            pltpu.VMEM((384, 1152), F32),
            pltpu.VMEM((blocks * VOL, LANES), F32),
            pltpu.VMEM((PAY, LANES), F32),
        ],
        name="halo",
    )(owner_dir, owner_slot, table, core, gd, rx0, rx1, ry0, ry1, rz0, rz1, at, rt, kgm, bias, p, active)

    swap = [(0, 1), (1, 0)]
    peers_ax = ("gx", "gy", "zl")
    peers = lax.axis_size(peers_ax)
    half = mine + lax.ppermute(other, "core", swap)
    spread = lax.all_to_all(half.reshape(peers, PAY // 2 // peers, LANES), peers_ax, 0, 0, tiled=True)
    share = jnp.sum(spread, axis=0)
    copies = jnp.broadcast_to(share[None], spread.shape)
    whole = lax.all_to_all(copies, peers_ax, 0, 0, tiled=True).reshape(PAY // 2, LANES)
    rest = lax.ppermute(whole, "core", swap)

    kernel_grad, bias_grad = pl.pallas_call(
        unpack_kernel,
        out_shape=(sds((27, channels, channels)), sds((1, channels))),
        in_specs=[SM, VM, VM],
        out_specs=(VM,) * 2,
        scratch_shapes=[pltpu.VMEM((PAY, LANES), F32)],
        name="unpack",
    )(core, whole, rest)
    return input_grad, kernel_grad, bias_grad.reshape(channels)


def solution(mesh):
    shape = mesh.devices.shape
    fine = Mesh(mesh.devices.reshape(shape[0], shape[1], shape[2] // 2, 2), AX)
    placed = (
        P(AX, None, None),
        P(AX, None, None),
        P(AX, None, None),
        P(),
        P(AX, None),
        P(AX, None),
        P(AX, None),
        P(AX),
    )
    return jax.shard_map(
        shards,
        mesh=fine,
        in_specs=placed,
        out_specs=(P(AX, None, None), P(), P()),
        check_vma=False,
    )
```

```python
import functools

import jax
import jax.numpy as jnp
import numpy as np
from jax import lax
from jax.experimental import pallas as pl
from jax.experimental.pallas import tpu as pltpu
from jax.sharding import Mesh, PartitionSpec as P

F32 = jnp.float32
BF16 = jnp.bfloat16
BS = 8
VOL = 512
LANES = 128
PAY = 1024
AX = ("zh", "x", "gy", "zl", "core")
AXX = ("zh", "x")
AXZ = ("zl", "core")

FACE = 64


def layout_of(blocks, listed):
    face = listed * FACE
    edge = listed * BS
    corner = -(-listed // 8) * 8
    y_rows = face + 2 * edge
    z_rows = face + 4 * edge + 4 * corner
    starts = [0]
    for size in (face, face, y_rows, y_rows, z_rows):
        starts.append(starts[-1] + size)
    total = starts[-1] + z_rows
    return dict(face=face, edge=edge, corner=corner, y_rows=y_rows, z_rows=z_rows,
                starts=starts, total=total)


def log2(n):
    return int(n).bit_length() - 1


def piece_table(blocks, listed):
    lay = layout_of(blocks, listed)
    face, edge, corner, starts = lay["face"], lay["edge"], lay["corner"], lay["starts"]
    table = np.zeros((27, 28), np.int32)
    for o in range(27):
        off = (o // 9 - 1, o // 3 % 3 - 1, o % 3 - 1)
        if off == (0, 0, 0):
            continue
        fixed = [7 if v == -1 else 0 for v in off]
        axis = 0 if off[0] else (1 if off[1] else 2)
        plane = [i for i in range(3) if i != axis]
        for d in range(27):
            own = (d // 9 - 1, d // 3 % 3 - 1, d % 3 - 1)
            if any(v != 0 and v != w for v, w in zip(own, off)):
                continue
            side = [(v + 1) // 2 for v in own]
            if own == (0, 0, 0):
                base, mult, strides = 0, VOL, {0: 64, 1: 8, 2: 1}
            elif own[2]:
                base = starts[4 + side[2]]
                if own[0] and own[1]:
                    base += face + 4 * edge + corner * (side[1] * 2 + side[0])
                    mult, strides = 1, {}
                elif own[0]:
                    base += face + edge * side[0]
                    mult, strides = 8, {1: 1}
                elif own[1]:
                    base += face + 2 * edge + edge * side[1]
                    mult, strides = 8, {0: 1}
                else:
                    mult, strides = 64, {0: 8, 1: 1}
            elif own[1]:
                base = starts[2 + side[1]]
                if own[0]:
                    base += face + edge * side[0]
                    mult, strides = 8, {2: 1}
                else:
                    mult, strides = 64, {0: 8, 2: 1}
            else:
                base = starts[side[0]]
                mult, strides = 64, {1: 8, 2: 1}
            for i in range(3):
                if off[i] != 0:
                    base += fixed[i] * strides.get(i, 0)
            s1 = strides[plane[0]] if off[plane[0]] == 0 else 1
            s2 = strides[plane[1]] if off[plane[1]] == 0 else 1
            table[o, d] = base | log2(mult) << 12 | log2(s1) << 16 | log2(s2) << 20
    return table.reshape(-1)


def split_hl(value, mask):
    high = value.astype(BF16).astype(F32)
    return jnp.where(mask, high, value - high)


def prep_kernel(core, send_h, cot_h, pre_h, act_h, gd, xs0, xs1, ys, zs, send, cot, pre, act, sems, asem, ssem):
    blocks = cot.shape[0]
    listed = send.shape[0]
    pairs = ((cot_h, cot, 0), (pre_h, pre, 1))
    copies = [[pltpu.make_async_copy(h.at[b], v.at[b], sems.at[b, i]) for h, v, i in pairs] for b in range(blocks)]
    act_copy = pltpu.make_async_copy(act_h, act, asem)
    send_copy = pltpu.make_async_copy(send_h, send, ssem)
    act_copy.start()
    for pair in copies:
        for copy in pair:
            copy.start()
    send_copy.start()
    act_copy.wait()
    for b in range(blocks):
        for copy in copies[b]:
            copy.wait()
        p = pre[b]
        s = 1.0 / (1.0 + jnp.exp(-p))
        m = act[b : b + 1, :].astype(F32)
        g = cot[b] * (s * (1.0 + p * (1.0 - s))) * m
        gd[b * VOL : (b + 1) * VOL, :] = jnp.concatenate([g, g], axis=0).T
    send_copy.wait()
    for i in range(listed):
        r0 = pl.multiple_of(jnp.minimum(send[i], blocks - 1) * VOL, VOL)
        for side in range(2):
            f = 7 * side
            (xs0, xs1)[side][i * 64 : (i + 1) * 64, :] = gd[pl.ds(r0 + f * 64, 64), :]
            for x in range(8):
                ys[side, i * 64 + x * 8 : i * 64 + x * 8 + 8, :] = gd[pl.ds(r0 + x * 64 + f * 8, 8), :]
            zs[side, i * 64 : (i + 1) * 64, :] = gd[pl.ds(r0 + f, 64, stride=8), :]


def pack_y_kernel(ys, rx0, rx1, after, out0, out1):
    face = ys.shape[1]
    listed = face // 64
    for side, out in ((0, out0), (1, out1)):
        f = 7 * side
        out[0:face, :] = ys[side]
        for j, rx in enumerate((rx0, rx1)):
            for s in range(listed):
                row = face + (j * listed + s) * 8
                out[row : row + 8, :] = rx[s * 64 + f * 8 : s * 64 + f * 8 + 8, :]


def pack_z_kernel(zs, rx0, rx1, ry0, ry1, after, out0, out1):
    face = zs.shape[1]
    listed = face // 64
    edge = listed * 8
    corner = -(-listed // 8) * 8
    for side, out in ((0, out0), (1, out1)):
        f = 7 * side
        out[0:face, :] = zs[side]
        for j, src in enumerate((rx0, rx1, ry0, ry1)):
            row = face + j * edge
            out[row : row + edge, :] = src[pl.ds(f, edge, stride=8), :]
        for j, src in enumerate((ry0, ry1)):
            for i in range(2):
                row = face + 4 * edge + corner * (2 * j + i)
                out[row : row + corner, :] = jnp.zeros((corner, LANES), F32)
                for s in range(listed):
                    at = face + i * edge + s * 8 + f
                    out[row + s : row + s + 1, :] = src[at : at + 1, :]


def interior_block(b, r0, gd, feat, act, at, p, kg_in, kg, rt, bias_in, bias, z):
    lane = lax.broadcasted_iota(jnp.int32, (VOL, LANES), 1) < 64
    rows = slice(r0, r0 + VOL)
    g = gd[b * VOL : (b + 1) * VOL, :]
    total = jnp.broadcast_to(jnp.sum(g, axis=0, keepdims=True), bias.shape)
    bias[...] = total if bias_in is None else bias_in[...] + total
    hl = split_hl(g, lane)
    row = lax.broadcasted_iota(jnp.int32, (VOL, LANES), 0)
    vy = (row // 8) % 8
    vz = row % 8
    for kz in (-1, 0, 1):
        if kz == 0:
            sz = hl
        elif kz == 1:
            sz = jnp.where(vz >= 1, pltpu.roll(hl, 1, 0), 0.0)
        else:
            sz = jnp.where(vz <= 6, pltpu.roll(hl, VOL - 1, 0), 0.0)
        for ky in (-1, 0, 1):
            if ky == 0:
                sy = sz
            elif ky == 1:
                sy = jnp.where(vy >= 1, pltpu.roll(sz, 8, 0), 0.0)
            else:
                sy = jnp.where(vy <= 6, pltpu.roll(sz, VOL - 8, 0), 0.0)
            c = (ky + 1) * 3 + kz + 1
            z[:, c * 128 : (c + 1) * 128] = sy.astype(BF16)

    f = feat * act[b : b + 1, :].astype(F32)
    ff = jnp.concatenate([f, f], axis=0)
    half = lax.broadcasted_iota(jnp.int32, (LANES, VOL), 0) < 64
    a = split_hl(ff, half)
    at[rows, :] = a.T
    zero = jnp.zeros((LANES, 64), F32)
    up = jnp.concatenate([zero, a[:, : VOL - 64]], axis=1)
    down = jnp.concatenate([a[:, 64:], zero], axis=1)
    a3 = jnp.concatenate([up, a, down], axis=0).astype(BF16)
    term = jnp.dot(a3, z[...], preferred_element_type=F32)
    kg[...] = term if kg_in is None else kg_in[...] + term
    p3 = lax.dot_general(z[...], rt[...], (((1,), (1,)), ((), ())), preferred_element_type=F32)
    p[rows, :] = p3[:, 128:256]
    p[r0 + 64 : r0 + VOL, :] += p3[: VOL - 64, 256:384]
    p[r0 : r0 + VOL - 64, :] += p3[64:, 0:128]


def fetch(part, feat_h, feat, sems):
    return [pltpu.make_async_copy(feat_h.at[b], feat.at[i], sems.at[i]) for i, b in enumerate(part)]


def first_kernel(part, gd, feat_h, act, kern_h, at, p, kg, rt, bias, z, feat, sems, kern, ksem):
    kern_copy = pltpu.make_async_copy(kern_h, kern, ksem)
    kern_copy.start()
    copies = fetch(part, feat_h, feat, sems)
    for copy in copies:
        copy.start()
    kern_copy.wait()
    for k in range(27):
        kx, c = k // 9, k % 9
        w = kern[k]
        wd = jnp.concatenate([w, w], axis=1)
        high = wd.astype(BF16)
        low = (wd - high.astype(F32)).astype(BF16)
        rt[kx * 128 : kx * 128 + 64, c * 128 : (c + 1) * 128] = high
        rt[kx * 128 + 64 : kx * 128 + 128, c * 128 : (c + 1) * 128] = low
    for i, b in enumerate(part):
        copies[i].wait()
        kgi, bi = (None, None) if i == 0 else (kg, bias)
        interior_block(b, i * VOL, gd, feat[i], act, at, p, kgi, kg, rt, bi, bias, z)


def next_kernel(part, held, *refs):
    gd, feat_h, act, rt, kg0, bias0 = refs[:6]
    earlier = refs[6 : 6 + 2 * held]
    at, p, kg, bias, z, feat, sems = refs[7 + 2 * held :]
    copies = fetch(part, feat_h, feat, sems)
    for copy in copies:
        copy.start()
    row = 0
    for i in range(held):
        n = earlier[2 * i].shape[0]
        at[row : row + n, :] = earlier[2 * i][...]
        p[row : row + n, :] = earlier[2 * i + 1][...]
        row += n
    for i, b in enumerate(part):
        copies[i].wait()
        kgi, bi = (kg0, bias0) if i == 0 else (kg, bias)
        interior_block(b, row + i * VOL, gd, feat[i], act, at, p, kgi, kg, rt, bi, bias, z)


def nt(a, b):
    return lax.dot_general(a, b, (((1,), (1,)), ((), ())), preferred_element_type=F32)


def tn(a, b):
    return lax.dot_general(a, b, (((0,), (0,)), ((), ())), preferred_element_type=F32)


def plane_pieces(axis, sign):
    out = []
    for o in range(27):
        off = (o // 9 - 1, o // 3 % 3 - 1, o % 3 - 1)
        if off[axis] == sign and all(off[i] == 0 for i in range(axis)):
            r, q = [off[i] for i in range(3) if i != axis]
            out.append((o, r, q))
    return out


def halo_kernel(scale, od, os_, tb, core, gd, rx0, rx1, ry0, ry1, rz0, rz1, at, rt, bias, p0, kg0,
                mine, other, pa, src, pb, pw, pay, kg):
    blocks = od.shape[0]
    row = 0
    for ref in (rx0, rx1, ry0, ry1, rz0, rz1):
        src[row : row + ref.shape[0], :] = ref[...]
        row += ref.shape[0]
    pa[...] = p0[...]
    kg[...] = kg0[...]
    lane64 = lax.broadcasted_iota(jnp.int32, (64, LANES), 1) < 64

    def plane(b, axis, sign):
        face = 0 if sign == -1 else 7
        pb[...] = jnp.zeros(pb.shape, F32)
        for o, r, q in plane_pieces(axis, sign):
            d = od[b, o]

            @pl.when(d != 27)
            def _(o=o, r=r, q=q, d=d):
                code = tb[o * 28 + d]
                base = (code & 4095) + (os_[b, o] << ((code >> 12) & 15))
                sr = (code >> 16) & 15
                sq = (code >> 20) & 15

                def fill(ref):
                    for i in range(8 if r == 0 else 1):
                        for j in range(8 if q == 0 else 1):
                            at_r = i + 1 if r == 0 else (0 if r == -1 else 9)
                            at_q = 8 + j if q == 0 else (7 if q == -1 else 16)
                            row = base + (i << sr) + (j << sq)
                            pb[at_r, at_q : at_q + 1, :] = ref[pl.ds(row, 1), :]

                pl.when(d == 13)(lambda: fill(gd))
                pl.when(d != 13)(lambda: fill(src))

        for kr in (-1, 0, 1):
            for kq in (-1, 0, 1):
                win = pb[1 - kr : 9 - kr, 8 - kq : 16 - kq, :].reshape(64, LANES)
                c = (kr + 1) * 3 + kq + 1
                pw[:, c * 128 : (c + 1) * 128] = split_hl(win, lane64).astype(BF16)
        r0 = b * VOL
        k = 1 - sign
        if axis == 0:
            rows = pl.ds(pl.multiple_of(r0 + face * 64, 64), 64)
            ap = at[rows, :].astype(BF16)
            span = slice(k * 128, (k + 1) * 128)
            kg[span, :] += tn(ap, pw[...])
            pa[rows, :] += nt(pw[...], rt[span, :])
        elif axis == 1:
            starts = [pl.multiple_of(r0 + x * 64 + face * 8, 8) for x in range(8)]
            ap = jnp.concatenate([at[pl.ds(s, 8), :] for s in starts], axis=0).astype(BF16)
            acc = jnp.zeros((64, LANES), F32)
            cols = slice(k * 384, (k + 1) * 384)
            for i in range(3):
                part = pw[:, i * 384 : (i + 1) * 384]
                kg[i * 128 : (i + 1) * 128, cols] += tn(ap, part)
                acc = acc + nt(part, rt[i * 128 : (i + 1) * 128, cols])
            for x, s in enumerate(starts):
                pa[pl.ds(s, 8), :] += acc[x * 8 : x * 8 + 8, :]
        else:
            rows = pl.ds(r0 + face, 64, stride=8)
            ap = at[rows, :].astype(BF16)
            acc = jnp.zeros((64, LANES), F32)
            for i in range(3):
                for j in range(3):
                    part = pw[:, (i * 3 + j) * 128 : (i * 3 + j + 1) * 128]
                    cols = slice((j * 3 + k) * 128, (j * 3 + k + 1) * 128)
                    kg[i * 128 : (i + 1) * 128, cols] += tn(ap, part)
                    acc = acc + nt(part, rt[i * 128 : (i + 1) * 128, cols])
            pa[rows, :] = pa[rows, :] + acc

    def block(b, carry):
        for axis in range(3):
            for sign in (-1, 1):
                found = od[b, plane_pieces(axis, sign)[0][0]] != 27
                for o, _, _ in plane_pieces(axis, sign)[1:]:
                    found = found | (od[b, o] != 27)

                @pl.when(found)
                def _(axis=axis, sign=sign):
                    plane(b, axis, sign)

        return carry

    lax.fori_loop(0, blocks, block, 0)

    for n in range(28):
        t, odd = n // 2, n % 2
        if n < 27:
            kx, c = n // 9, n % 9
            lo, hi = c * 128, (c + 1) * 128
            u = kg[kx * 128 : kx * 128 + 64, lo:hi] + kg[kx * 128 + 64 : kx * 128 + 128, lo:hi]
            u = u + pltpu.roll(u, 64, 1)
        else:
            first = lax.broadcasted_iota(jnp.int32, (64, LANES), 0) == 0
            u = jnp.where(first, jnp.broadcast_to(bias[0:1, :], (64, LANES)), 0.0)
        if odd:
            pay[t * 64 : (t + 1) * 64, :] = jnp.where(lane64, held, u) * scale
        held = u
    pay[14 * 64 :, :] = jnp.zeros((PAY - 14 * 64, LANES), F32)
    me = core[0]
    mine[...] = pay[pl.ds(pl.multiple_of(me * (PAY // 2), PAY // 2), PAY // 2), :]
    other[...] = pay[pl.ds(pl.multiple_of((1 - me) * (PAY // 2), PAY // 2), PAY // 2), :]


def finish_kernel(pa, act, ig):
    for b in range(act.shape[0]):
        og = pa[b * VOL : (b + 1) * VOL, :]
        og = (og + pltpu.roll(og, 64, 1)).T
        ig[b] = og[:64, :] * act[b : b + 1, :].astype(F32)


def unpack_kernel(core, mine, other, kout, bout, pay):
    me = core[0]
    pay[pl.ds(pl.multiple_of(me * (PAY // 2), PAY // 2), PAY // 2), :] = mine[...]
    pay[pl.ds(pl.multiple_of((1 - me) * (PAY // 2), PAY // 2), PAY // 2), :] = other[...]
    for t in range(14):
        tile = pay[t * 64 : (t + 1) * 64, :]
        turned = pltpu.roll(tile, 64, 1)
        kout[2 * t] = tile[:, :64]
        if t < 13:
            kout[2 * t + 1] = turned[:, :64]
        else:
            bout[...] = turned[0:1, :64]


VM = pl.BlockSpec(memory_space=pltpu.VMEM)
SM = pl.BlockSpec(memory_space=pltpu.SMEM)
ANY = pl.BlockSpec(memory_space=pl.ANY)
ROOM = pltpu.CompilerParams(vmem_limit_bytes=32 * 2**20)


def sds(shape, dtype=F32):
    return jax.ShapeDtypeStruct(shape, dtype)


def both_ways(low, high, axis):
    n = lax.axis_size(axis)
    up = lax.ppermute(high, axis, [(i, i + 1) for i in range(n - 1)])
    down = lax.ppermute(low, axis, [(i + 1, i) for i in range(n - 1)])
    return up, down


def vm(shape, dtype=F32):
    return pltpu.VMEM(shape, dtype)


def local(x):
    return pltpu.with_memory_space_constraint(x, pltpu.VMEM)


def far(x):
    return pltpu.with_memory_space_constraint(x, pltpu.HBM)


def shards(features, preact, cotangent, kernel, active, owner_dir, owner_slot, send_list):
    blocks, channels, volume = features.shape
    listed = send_list.shape[0]
    lay = layout_of(blocks, listed)
    face, yr, zr = lay["face"], lay["y_rows"], lay["z_rows"]
    rows = blocks * VOL
    devices = lax.axis_size(AX)
    core = lax.axis_index("core").astype(jnp.int32).reshape(1)
    scale = float((volume * blocks * devices) ** -0.5)

    gd, xs0, xs1, ys, zs = pl.pallas_call(
        prep_kernel,
        out_shape=(vm((rows, LANES)), vm((face, LANES)), vm((face, LANES)), vm((2, face, LANES)), vm((2, face, LANES))),
        in_specs=[SM] + [ANY] * 4,
        out_specs=(VM,) * 5,
        scratch_shapes=[
            pltpu.SMEM((listed,), jnp.int32),
            pltpu.VMEM((blocks, channels, VOL), F32),
            pltpu.VMEM((blocks, channels, VOL), F32),
            pltpu.VMEM((blocks, VOL), jnp.int32),
            pltpu.SemaphoreType.DMA((blocks, 2)),
            pltpu.SemaphoreType.DMA,
            pltpu.SemaphoreType.DMA,
        ],
        name="prep", compiler_params=ROOM,
    )(core, far(send_list), far(cotangent), far(preact), far(active))
    rx0, rx1 = both_ways(xs0, xs1, AXX)

    third = max(blocks // 4, 1)
    parts = (range(third), range(third, 2 * third), range(2 * third, blocks))

    def scratch(part):
        return [
            pltpu.VMEM((VOL, 1152), BF16),
            pltpu.VMEM((max(len(part), 1), channels, VOL), F32),
            pltpu.SemaphoreType.DMA((max(len(part), 1),)),
        ]

    wide = (384, 1152)
    n0 = len(parts[0]) * VOL
    at0, p0, kg, rt, bias = pl.pallas_call(
        functools.partial(first_kernel, parts[0]),
        in_specs=[VM, ANY, VM, ANY],
        out_specs=(VM,) * 5,
        out_shape=(vm((n0, LANES)), vm((n0, LANES)), vm(wide), vm(wide, BF16), vm((8, LANES))),
        scratch_shapes=scratch(parts[0]) + [pltpu.VMEM((27, channels, channels), F32), pltpu.SemaphoreType.DMA],
        name="interior0", compiler_params=ROOM,
    )(local(gd), far(features), active, far(kernel))

    def more(part, earlier, kg, bias, after, name):
        n = len(part) * VOL + sum(e.shape[0] for e in earlier[::2])
        return pl.pallas_call(
            functools.partial(next_kernel, part, len(earlier) // 2),
            in_specs=[VM, ANY] + [VM] * (4 + len(earlier)) + [ANY],
            out_specs=(VM,) * 4,
            out_shape=(vm((n, LANES)), vm((n, LANES)), vm(wide), vm((8, LANES))),
            scratch_shapes=scratch(part),
            name=name, compiler_params=ROOM,
        )(local(gd), far(features), active, local(rt), local(kg), local(bias), *[local(e) for e in earlier], after)

    ys0, ys1 = pl.pallas_call(
        pack_y_kernel, out_shape=(vm((yr, LANES)),) * 2, in_specs=[VM] * 3 + [ANY], out_specs=(VM,) * 2,
        name="pack_y", compiler_params=ROOM,
    )(local(ys), local(rx0), local(rx1), bias)
    ry0, ry1 = both_ways(ys0, ys1, "gy")
    at1, p1, kg, bias = more(parts[1], (), kg, bias, ys0, "interior1")
    zs0, zs1 = pl.pallas_call(
        pack_z_kernel, out_shape=(vm((zr, LANES)),) * 2, in_specs=[VM] * 5 + [ANY], out_specs=(VM,) * 2,
        name="pack_z", compiler_params=ROOM,
    )(local(zs), local(rx0), local(rx1), local(ry0), local(ry1), bias)
    rz0, rz1 = both_ways(zs0, zs1, AXZ)
    at, p, kg, bias = more(parts[2], (at0, p0, at1, p1), kg, bias, zs0, "interior2")

    table = jnp.asarray(piece_table(blocks, listed))
    mine, other, p = pl.pallas_call(
        functools.partial(halo_kernel, scale),
        out_shape=(vm((PAY // 2, LANES)), vm((PAY // 2, LANES)), vm((rows, LANES))),
        in_specs=[SM] * 4 + [VM] * 12,
        out_specs=(VM,) * 3,
        scratch_shapes=[
            pltpu.VMEM((lay["total"], LANES), F32),
            pltpu.VMEM((10, 24, LANES), F32),
            pltpu.VMEM((64, 1152), BF16),
            pltpu.VMEM((PAY, LANES), F32),
            pltpu.VMEM((384, 1152), F32),
        ],
        name="halo", compiler_params=ROOM,
    )(owner_dir, owner_slot, table, core, local(gd), local(rx0), local(rx1), local(ry0), local(ry1),
      local(rz0), local(rz1), local(at), local(rt), local(bias), local(p), local(kg))

    swap = [(0, 1), (1, 0)]
    arrived = lax.ppermute(other, "core", swap)
    input_grad = pl.pallas_call(
        finish_kernel, out_shape=sds((blocks, channels, VOL)), in_specs=[VM] * 2, out_specs=VM, name="finish", compiler_params=ROOM,
    )(local(p), active)
    half = mine + arrived
    plane, depth = lax.axis_size(("x", "gy")), lax.axis_size(("zh", "zl"))
    spread = lax.all_to_all(half.reshape(plane, PAY // 2 // plane, LANES), ("x", "gy"), 0, 0, tiled=True)
    share = jnp.sum(spread, axis=0)
    share = lax.all_to_all(jnp.broadcast_to(share[None], (depth,) + share.shape), ("zh", "zl"), 0, 0, tiled=True)
    share = jnp.sum(share, axis=0)
    whole = lax.all_to_all(jnp.broadcast_to(share[None], spread.shape), ("x", "gy"), 0, 0, tiled=True)
    whole = whole.reshape(PAY // 2, LANES)
    rest = lax.ppermute(whole, "core", swap)

    kernel_grad, bias_grad = pl.pallas_call(
        unpack_kernel,
        out_shape=(sds((27, channels, channels)), sds((1, channels))),
        in_specs=[SM, VM, VM],
        out_specs=(VM,) * 2,
        scratch_shapes=[pltpu.VMEM((PAY, LANES), F32)],
        name="unpack", compiler_params=ROOM,
    )(core, local(whole), local(rest))
    return input_grad, kernel_grad, bias_grad.reshape(channels)


def solution(mesh):
    shape = mesh.devices.shape
    fine = Mesh(mesh.devices.reshape(2, shape[0] // 2, shape[1], shape[2] // 2, 2), AX)
    placed = (
        P(AX, None, None),
        P(AX, None, None),
        P(AX, None, None),
        P(),
        P(AX, None),
        P(AX, None),
        P(AX, None),
        P(AX),
    )
    return jax.shard_map(
        shards,
        mesh=fine,
        in_specs=placed,
        out_specs=(P(AX, None, None), P(), P()),
        check_vma=False,
    )
```

```python
import functools

import jax
import jax.numpy as jnp
import numpy as np
from jax import lax
from jax.experimental import pallas as pl
from jax.experimental.pallas import tpu as pltpu
from jax.sharding import Mesh, PartitionSpec as P

F32 = jnp.float32
BF16 = jnp.bfloat16
BS = 8
VOL = 512
LANES = 128
PAY = 896
AX = ("zh", "x", "gy", "zl", "core")
AXX = ("zh", "x")
AXZ = ("zl", "core")

FACE = 64


def layout_of(blocks, listed):
    face = listed * FACE
    edge = listed * BS
    corner = -(-listed // 8) * 8
    y_rows = face + 2 * edge
    z_rows = face + 4 * edge + 4 * corner
    starts = [0]
    for size in (face, face, y_rows, y_rows, z_rows):
        starts.append(starts[-1] + size)
    total = starts[-1] + z_rows
    return dict(face=face, edge=edge, corner=corner, y_rows=y_rows, z_rows=z_rows,
                starts=starts, total=total)


def log2(n):
    return int(n).bit_length() - 1


def piece_table(blocks, listed):
    lay = layout_of(blocks, listed)
    face, edge, corner, starts = lay["face"], lay["edge"], lay["corner"], lay["starts"]
    table = np.zeros((27, 28), np.int32)
    for o in range(27):
        off = (o // 9 - 1, o // 3 % 3 - 1, o % 3 - 1)
        if off == (0, 0, 0):
            continue
        fixed = [7 if v == -1 else 0 for v in off]
        axis = 0 if off[0] else (1 if off[1] else 2)
        plane = [i for i in range(3) if i != axis]
        for d in range(27):
            own = (d // 9 - 1, d // 3 % 3 - 1, d % 3 - 1)
            if any(v != 0 and v != w for v, w in zip(own, off)):
                continue
            side = [(v + 1) // 2 for v in own]
            if own == (0, 0, 0):
                base, mult, strides = 0, VOL, {0: 64, 1: 8, 2: 1}
            elif own[2]:
                base = starts[4 + side[2]]
                if own[0] and own[1]:
                    base += face + 4 * edge + corner * (side[1] * 2 + side[0])
                    mult, strides = 1, {}
                elif own[0]:
                    base += face + edge * side[0]
                    mult, strides = 8, {1: 1}
                elif own[1]:
                    base += face + 2 * edge + edge * side[1]
                    mult, strides = 8, {0: 1}
                else:
                    mult, strides = 64, {0: 8, 1: 1}
            elif own[1]:
                base = starts[2 + side[1]]
                if own[0]:
                    base += face + edge * side[0]
                    mult, strides = 8, {2: 1}
                else:
                    mult, strides = 64, {0: 8, 2: 1}
            else:
                base = starts[side[0]]
                mult, strides = 64, {1: 8, 2: 1}
            for i in range(3):
                if off[i] != 0:
                    base += fixed[i] * strides.get(i, 0)
            s1 = strides[plane[0]] if off[plane[0]] == 0 else 1
            s2 = strides[plane[1]] if off[plane[1]] == 0 else 1
            table[o, d] = base | log2(mult) << 12 | log2(s1) << 16 | log2(s2) << 20
    return table.reshape(-1)


def split_hl(value, mask):
    high = value.astype(BF16).astype(F32)
    return jnp.where(mask, high, value - high)


def pack_rows(ref, out):
    n = out.shape[0]
    left = lax.broadcasted_iota(jnp.int32, (n, LANES), 1) < 64
    out[...] = jnp.where(left, ref[0:n, :], ref[n : 2 * n, :])


def unpack_rows(ref, out, start=0):
    n = ref.shape[0]
    left = lax.broadcasted_iota(jnp.int32, (n, LANES), 1) < 64
    v = ref[...]
    w = pltpu.roll(v, 64, 1)
    out[start : start + n, :] = jnp.where(left, v, w)
    out[start + n : start + 2 * n, :] = jnp.where(left, w, v)


def prep_kernel(core, send_h, cot_h, pre_h, act_h, gd, xs0, xs1, ys, zs, send, cot, pre, act, sems, asem, ssem, xf):
    blocks = cot.shape[0]
    listed = send.shape[0]
    pairs = ((cot_h, cot, 0), (pre_h, pre, 1))
    copies = [[pltpu.make_async_copy(h.at[b], v.at[b], sems.at[b, i]) for h, v, i in pairs] for b in range(blocks)]
    act_copy = pltpu.make_async_copy(act_h, act, asem)
    send_copy = pltpu.make_async_copy(send_h, send, ssem)
    act_copy.start()
    for pair in copies:
        for copy in pair:
            copy.start()
    send_copy.start()
    act_copy.wait()
    for b in range(blocks):
        for copy in copies[b]:
            copy.wait()
        p = pre[b]
        s = 1.0 / (1.0 + jnp.exp(-p))
        m = act[b : b + 1, :].astype(F32)
        g = cot[b] * (s * (1.0 + p * (1.0 - s))) * m
        gd[b * VOL : (b + 1) * VOL, :] = jnp.concatenate([g, g], axis=0).T
    send_copy.wait()
    for i in range(listed):
        r0 = pl.multiple_of(jnp.minimum(send[i], blocks - 1) * VOL, VOL)
        for side in range(2):
            f = 7 * side
            xf[side, i * 64 : (i + 1) * 64, :] = gd[pl.ds(r0 + f * 64, 64), :]
            for x in range(8):
                ys[side, i * 64 + x * 8 : i * 64 + x * 8 + 8, :] = gd[pl.ds(r0 + x * 64 + f * 8, 8), :]
            zs[side, i * 64 : (i + 1) * 64, :] = gd[pl.ds(r0 + f, 64, stride=8), :]
    pack_rows(xf.at[0], xs0)
    pack_rows(xf.at[1], xs1)


def pack_y_kernel(ys, rx0, rx1, after, out0, out1, xf, yf):
    face = ys.shape[1]
    listed = face // 64
    unpack_rows(rx0, xf.at[0])
    unpack_rows(rx1, xf.at[1])
    for side, out in ((0, out0), (1, out1)):
        f = 7 * side
        yf[0:face, :] = ys[side]
        for j in range(2):
            for s in range(listed):
                row = face + (j * listed + s) * 8
                yf[row : row + 8, :] = xf[j, s * 64 + f * 8 : s * 64 + f * 8 + 8, :]
        pack_rows(yf, out)


def pack_z_kernel(zs, rx0, rx1, ry0, ry1, after, out0, out1, x0, x1, y0, y1, zf):
    face = zs.shape[1]
    listed = face // 64
    edge = listed * 8
    corner = -(-listed // 8) * 8
    for src, full in ((rx0, x0), (rx1, x1), (ry0, y0), (ry1, y1)):
        unpack_rows(src, full)
    for side, out in ((0, out0), (1, out1)):
        f = 7 * side
        zf[0:face, :] = zs[side]
        for j, src in enumerate((x0, x1, y0, y1)):
            row = face + j * edge
            zf[row : row + edge, :] = src[pl.ds(f, edge, stride=8), :]
        for j, src in enumerate((y0, y1)):
            for i in range(2):
                row = face + 4 * edge + corner * (2 * j + i)
                zf[row : row + corner, :] = jnp.zeros((corner, LANES), F32)
                for s in range(listed):
                    at = face + i * edge + s * 8 + f
                    zf[row + s : row + s + 1, :] = src[at : at + 1, :]
        pack_rows(zf, out)


def interior_block(b, r0, gd, feat, act, at, p, kg_in, kg, rt, bias_in, bias, z):
    lane = lax.broadcasted_iota(jnp.int32, (VOL, LANES), 1) < 64
    rows = slice(r0, r0 + VOL)
    g = gd[b * VOL : (b + 1) * VOL, :]
    total = jnp.broadcast_to(jnp.sum(g, axis=0, keepdims=True), bias.shape)
    bias[...] = total if bias_in is None else bias_in[...] + total
    hl = split_hl(g, lane)
    row = lax.broadcasted_iota(jnp.int32, (VOL, LANES), 0)
    vy = (row // 8) % 8
    vz = row % 8
    for kz in (-1, 0, 1):
        if kz == 0:
            sz = hl
        elif kz == 1:
            sz = jnp.where(vz >= 1, pltpu.roll(hl, 1, 0), 0.0)
        else:
            sz = jnp.where(vz <= 6, pltpu.roll(hl, VOL - 1, 0), 0.0)
        for ky in (-1, 0, 1):
            if ky == 0:
                sy = sz
            elif ky == 1:
                sy = jnp.where(vy >= 1, pltpu.roll(sz, 8, 0), 0.0)
            else:
                sy = jnp.where(vy <= 6, pltpu.roll(sz, VOL - 8, 0), 0.0)
            c = (ky + 1) * 3 + kz + 1
            z[:, c * 128 : (c + 1) * 128] = sy.astype(BF16)

    f = feat * act[b : b + 1, :].astype(F32)
    ff = jnp.concatenate([f, f], axis=0)
    half = lax.broadcasted_iota(jnp.int32, (LANES, VOL), 0) < 64
    a = split_hl(ff, half)
    at[rows, :] = a.T
    zero = jnp.zeros((LANES, 64), F32)
    up = jnp.concatenate([zero, a[:, : VOL - 64]], axis=1)
    down = jnp.concatenate([a[:, 64:], zero], axis=1)
    a3 = jnp.concatenate([up, a, down], axis=0).astype(BF16)
    term = jnp.dot(a3, z[...], preferred_element_type=F32)
    kg[...] = term if kg_in is None else kg_in[...] + term
    p3 = lax.dot_general(z[...], rt[...], (((1,), (1,)), ((), ())), preferred_element_type=F32)
    p[rows, :] = p3[:, 128:256]
    p[r0 + 64 : r0 + VOL, :] += p3[: VOL - 64, 256:384]
    p[r0 : r0 + VOL - 64, :] += p3[64:, 0:128]


def fetch(part, feat_h, feat, sems):
    return [pltpu.make_async_copy(feat_h.at[b], feat.at[i], sems.at[i]) for i, b in enumerate(part)]


def first_kernel(part, gd, feat_h, act, kern_h, at, p, kg, rt, bias, z, feat, sems, kern, ksem):
    kern_copy = pltpu.make_async_copy(kern_h, kern, ksem)
    kern_copy.start()
    copies = fetch(part, feat_h, feat, sems)
    for copy in copies:
        copy.start()
    kern_copy.wait()
    for k in range(27):
        kx, c = k // 9, k % 9
        w = kern[k]
        wd = jnp.concatenate([w, w], axis=1)
        high = wd.astype(BF16)
        low = (wd - high.astype(F32)).astype(BF16)
        rt[kx * 128 : kx * 128 + 64, c * 128 : (c + 1) * 128] = high
        rt[kx * 128 + 64 : kx * 128 + 128, c * 128 : (c + 1) * 128] = low
    for i, b in enumerate(part):
        copies[i].wait()
        kgi, bi = (None, None) if i == 0 else (kg, bias)
        interior_block(b, i * VOL, gd, feat[i], act, at, p, kgi, kg, rt, bi, bias, z)


def next_kernel(part, held, *refs):
    gd, feat_h, act, rt, kg0, bias0 = refs[:6]
    earlier = refs[6 : 6 + 2 * held]
    at, p, kg, bias, z, feat, sems = refs[7 + 2 * held :]
    copies = fetch(part, feat_h, feat, sems)
    for copy in copies:
        copy.start()
    row = 0
    for i in range(held):
        n = earlier[2 * i].shape[0]
        at[row : row + n, :] = earlier[2 * i][...]
        p[row : row + n, :] = earlier[2 * i + 1][...]
        row += n
    for i, b in enumerate(part):
        copies[i].wait()
        kgi, bi = (kg0, bias0) if i == 0 else (kg, bias)
        interior_block(b, row + i * VOL, gd, feat[i], act, at, p, kgi, kg, rt, bi, bias, z)


def nt(a, b):
    return lax.dot_general(a, b, (((1,), (1,)), ((), ())), preferred_element_type=F32)


def tn(a, b):
    return lax.dot_general(a, b, (((0,), (0,)), ((), ())), preferred_element_type=F32)


def plane_pieces(axis, sign):
    out = []
    for o in range(27):
        off = (o // 9 - 1, o // 3 % 3 - 1, o % 3 - 1)
        if off[axis] == sign and all(off[i] == 0 for i in range(axis)):
            r, q = [off[i] for i in range(3) if i != axis]
            out.append((o, r, q))
    return out


def halo_kernel(scale, od, os_, tb, core, gd, rx0, rx1, ry0, ry1, rz0, rz1, at, rt, bias, p0, kg0,
                mine, other, pa, src, pb, pw, pay, kg):
    blocks = od.shape[0]
    row = 0
    for ref in (rx0, rx1, ry0, ry1, rz0, rz1):
        unpack_rows(ref, src, row)
        row += 2 * ref.shape[0]
    pa[...] = p0[...]
    kg[...] = kg0[...]
    lane64 = lax.broadcasted_iota(jnp.int32, (64, LANES), 1) < 64

    def plane(b, axis, sign):
        face = 0 if sign == -1 else 7
        pb[...] = jnp.zeros(pb.shape, F32)
        for o, r, q in plane_pieces(axis, sign):
            d = od[b, o]

            @pl.when(d != 27)
            def _(o=o, r=r, q=q, d=d):
                code = tb[o * 28 + d]
                base = (code & 4095) + (os_[b, o] << ((code >> 12) & 15))
                sr = (code >> 16) & 15
                sq = (code >> 20) & 15

                def fill(ref):
                    for i in range(8 if r == 0 else 1):
                        for j in range(8 if q == 0 else 1):
                            at_r = i + 1 if r == 0 else (0 if r == -1 else 9)
                            at_q = 8 + j if q == 0 else (7 if q == -1 else 16)
                            row = base + (i << sr) + (j << sq)
                            pb[at_r, at_q : at_q + 1, :] = ref[pl.ds(row, 1), :]

                pl.when(d == 13)(lambda: fill(gd))
                pl.when(d != 13)(lambda: fill(src))

        for kr in (-1, 0, 1):
            for kq in (-1, 0, 1):
                win = pb[1 - kr : 9 - kr, 8 - kq : 16 - kq, :].reshape(64, LANES)
                c = (kr + 1) * 3 + kq + 1
                pw[:, c * 128 : (c + 1) * 128] = split_hl(win, lane64).astype(BF16)
        r0 = b * VOL
        k = 1 - sign
        if axis == 0:
            rows = pl.ds(pl.multiple_of(r0 + face * 64, 64), 64)
            ap = at[rows, :].astype(BF16)
            span = slice(k * 128, (k + 1) * 128)
            kg[span, :] += tn(ap, pw[...])
            pa[rows, :] += nt(pw[...], rt[span, :])
        elif axis == 1:
            starts = [pl.multiple_of(r0 + x * 64 + face * 8, 8) for x in range(8)]
            ap = jnp.concatenate([at[pl.ds(s, 8), :] for s in starts], axis=0).astype(BF16)
            acc = jnp.zeros((64, LANES), F32)
            cols = slice(k * 384, (k + 1) * 384)
            for i in range(3):
                part = pw[:, i * 384 : (i + 1) * 384]
                kg[i * 128 : (i + 1) * 128, cols] += tn(ap, part)
                acc = acc + nt(part, rt[i * 128 : (i + 1) * 128, cols])
            for x, s in enumerate(starts):
                pa[pl.ds(s, 8), :] += acc[x * 8 : x * 8 + 8, :]
        else:
            rows = pl.ds(r0 + face, 64, stride=8)
            ap = at[rows, :].astype(BF16)
            acc = jnp.zeros((64, LANES), F32)
            for i in range(3):
                for j in range(3):
                    part = pw[:, (i * 3 + j) * 128 : (i * 3 + j + 1) * 128]
                    cols = slice((j * 3 + k) * 128, (j * 3 + k + 1) * 128)
                    kg[i * 128 : (i + 1) * 128, cols] += tn(ap, part)
                    acc = acc + nt(part, rt[i * 128 : (i + 1) * 128, cols])
            pa[rows, :] = pa[rows, :] + acc

    def block(b, carry):
        for axis in range(3):
            for sign in (-1, 1):
                found = od[b, plane_pieces(axis, sign)[0][0]] != 27
                for o, _, _ in plane_pieces(axis, sign)[1:]:
                    found = found | (od[b, o] != 27)

                @pl.when(found)
                def _(axis=axis, sign=sign):
                    plane(b, axis, sign)

        return carry

    lax.fori_loop(0, blocks, block, 0)

    for n in range(28):
        t, odd = n // 2, n % 2
        if n < 27:
            kx, c = n // 9, n % 9
            lo, hi = c * 128, (c + 1) * 128
            u = kg[kx * 128 : kx * 128 + 64, lo:hi] + kg[kx * 128 + 64 : kx * 128 + 128, lo:hi]
            u = u + pltpu.roll(u, 64, 1)
        else:
            first = lax.broadcasted_iota(jnp.int32, (64, LANES), 0) == 0
            u = jnp.where(first, jnp.broadcast_to(bias[0:1, :], (64, LANES)), 0.0)
        if odd:
            pay[t * 64 : (t + 1) * 64, :] = jnp.where(lane64, held, u) * scale
        held = u
    me = core[0]
    mine[...] = pay[pl.ds(pl.multiple_of(me * (PAY // 2), PAY // 2), PAY // 2), :]
    other[...] = pay[pl.ds(pl.multiple_of((1 - me) * (PAY // 2), PAY // 2), PAY // 2), :]


def finish_kernel(pa, act, ig):
    for b in range(act.shape[0]):
        og = pa[b * VOL : (b + 1) * VOL, :]
        og = (og + pltpu.roll(og, 64, 1)).T
        ig[b] = og[:64, :] * act[b : b + 1, :].astype(F32)


def unpack_kernel(core, mine, other, kout, bout, pay):
    me = core[0]
    pay[pl.ds(pl.multiple_of(me * (PAY // 2), PAY // 2), PAY // 2), :] = mine[...]
    pay[pl.ds(pl.multiple_of((1 - me) * (PAY // 2), PAY // 2), PAY // 2), :] = other[...]
    for t in range(14):
        tile = pay[t * 64 : (t + 1) * 64, :]
        turned = pltpu.roll(tile, 64, 1)
        kout[2 * t] = tile[:, :64]
        if t < 13:
            kout[2 * t + 1] = turned[:, :64]
        else:
            bout[...] = turned[0:1, :64]


VM = pl.BlockSpec(memory_space=pltpu.VMEM)
SM = pl.BlockSpec(memory_space=pltpu.SMEM)
ANY = pl.BlockSpec(memory_space=pl.ANY)
ROOM = pltpu.CompilerParams(vmem_limit_bytes=32 * 2**20)


def sds(shape, dtype=F32):
    return jax.ShapeDtypeStruct(shape, dtype)


def both_ways(low, high, axis):
    n = lax.axis_size(axis)
    up = lax.ppermute(high, axis, [(i, i + 1) for i in range(n - 1)])
    down = lax.ppermute(low, axis, [(i + 1, i) for i in range(n - 1)])
    return up, down


def vm(shape, dtype=F32):
    return pltpu.VMEM(shape, dtype)


def local(x):
    return pltpu.with_memory_space_constraint(x, pltpu.VMEM)


def far(x):
    return pltpu.with_memory_space_constraint(x, pltpu.HBM)


def shards(features, preact, cotangent, kernel, active, owner_dir, owner_slot, send_list):
    blocks, channels, volume = features.shape
    listed = send_list.shape[0]
    lay = layout_of(blocks, listed)
    face, yr, zr = lay["face"], lay["y_rows"], lay["z_rows"]
    rows = blocks * VOL
    devices = lax.axis_size(AX)
    core = lax.axis_index("core").astype(jnp.int32).reshape(1)
    scale = float((volume * blocks * devices) ** -0.5)

    gd, xs0, xs1, ys, zs = pl.pallas_call(
        prep_kernel,
        out_shape=(vm((rows, LANES)), vm((face // 2, LANES)), vm((face // 2, LANES)), vm((2, face, LANES)), vm((2, face, LANES))),
        in_specs=[SM] + [ANY] * 4,
        out_specs=(VM,) * 5,
        scratch_shapes=[
            pltpu.SMEM((listed,), jnp.int32),
            pltpu.VMEM((blocks, channels, VOL), F32),
            pltpu.VMEM((blocks, channels, VOL), F32),
            pltpu.VMEM((blocks, VOL), jnp.int32),
            pltpu.SemaphoreType.DMA((blocks, 2)),
            pltpu.SemaphoreType.DMA,
            pltpu.SemaphoreType.DMA,
            pltpu.VMEM((2, face, LANES), F32),
        ],
        name="prep", compiler_params=ROOM,
    )(core, far(send_list), far(cotangent), far(preact), far(active))
    rx0, rx1 = both_ways(xs0, xs1, AXX)

    third = max(blocks // 4, 1)
    parts = (range(third), range(third, 2 * third), range(2 * third, blocks))

    def scratch(part):
        return [
            pltpu.VMEM((VOL, 1152), BF16),
            pltpu.VMEM((max(len(part), 1), channels, VOL), F32),
            pltpu.SemaphoreType.DMA((max(len(part), 1),)),
        ]

    wide = (384, 1152)
    n0 = len(parts[0]) * VOL
    at0, p0, kg, rt, bias = pl.pallas_call(
        functools.partial(first_kernel, parts[0]),
        in_specs=[VM, ANY, VM, ANY],
        out_specs=(VM,) * 5,
        out_shape=(vm((n0, LANES)), vm((n0, LANES)), vm(wide), vm(wide, BF16), vm((8, LANES))),
        scratch_shapes=scratch(parts[0]) + [pltpu.VMEM((27, channels, channels), F32), pltpu.SemaphoreType.DMA],
        name="interior0", compiler_params=ROOM,
    )(local(gd), far(features), active, far(kernel))

    def more(part, earlier, kg, bias, after, name):
        n = len(part) * VOL + sum(e.shape[0] for e in earlier[::2])
        return pl.pallas_call(
            functools.partial(next_kernel, part, len(earlier) // 2),
            in_specs=[VM, ANY] + [VM] * (4 + len(earlier)) + [ANY],
            out_specs=(VM,) * 4,
            out_shape=(vm((n, LANES)), vm((n, LANES)), vm(wide), vm((8, LANES))),
            scratch_shapes=scratch(part),
            name=name, compiler_params=ROOM,
        )(local(gd), far(features), active, local(rt), local(kg), local(bias), *[local(e) for e in earlier], after)

    ys0, ys1 = pl.pallas_call(
        pack_y_kernel, out_shape=(vm((yr // 2, LANES)),) * 2,
        scratch_shapes=[pltpu.VMEM((2, face, LANES), F32), pltpu.VMEM((yr, LANES), F32)],
        in_specs=[VM] * 3 + [ANY], out_specs=(VM,) * 2,
        name="pack_y", compiler_params=ROOM,
    )(local(ys), local(rx0), local(rx1), bias)
    ry0, ry1 = both_ways(ys0, ys1, "gy")
    at1, p1, kg, bias = more(parts[1], (), kg, bias, ys0, "interior1")
    zs0, zs1 = pl.pallas_call(
        pack_z_kernel, out_shape=(vm((zr // 2, LANES)),) * 2,
        scratch_shapes=[pltpu.VMEM((n, LANES), F32) for n in (face, face, yr, yr, zr)],
        in_specs=[VM] * 5 + [ANY], out_specs=(VM,) * 2,
        name="pack_z", compiler_params=ROOM,
    )(local(zs), local(rx0), local(rx1), local(ry0), local(ry1), bias)
    rz0, rz1 = both_ways(zs0, zs1, AXZ)
    at, p, kg, bias = more(parts[2], (at0, p0, at1, p1), kg, bias, zs0, "interior2")

    table = jnp.asarray(piece_table(blocks, listed))
    mine, other, p = pl.pallas_call(
        functools.partial(halo_kernel, scale),
        out_shape=(vm((PAY // 2, LANES)), vm((PAY // 2, LANES)), vm((rows, LANES))),
        in_specs=[SM] * 4 + [VM] * 12,
        out_specs=(VM,) * 3,
        scratch_shapes=[
            pltpu.VMEM((lay["total"], LANES), F32),
            pltpu.VMEM((10, 24, LANES), F32),
            pltpu.VMEM((64, 1152), BF16),
            pltpu.VMEM((PAY, LANES), F32),
            pltpu.VMEM((384, 1152), F32),
        ],
        name="halo", compiler_params=ROOM,
    )(owner_dir, owner_slot, table, core, local(gd), local(rx0), local(rx1), local(ry0), local(ry1),
      local(rz0), local(rz1), local(at), local(rt), local(bias), local(p), local(kg))

    swap = [(0, 1), (1, 0)]
    arrived = lax.ppermute(other, "core", swap)
    input_grad = pl.pallas_call(
        finish_kernel, out_shape=sds((blocks, channels, VOL)), in_specs=[VM] * 2, out_specs=VM, name="finish", compiler_params=ROOM,
    )(local(p), active)
    half = mine + arrived
    plane, depth = lax.axis_size(("x", "gy")), lax.axis_size(("zh", "zl"))
    chunk = PAY // 2 // plane // 2

    def trade(x, count, axes):
        x = lax.all_to_all(x.reshape(count * chunk, 2, LANES), axes, 0, 0, tiled=True)
        return x.reshape(count, chunk, 2, LANES)

    def copies(x, count):
        return jnp.broadcast_to(x[None], (count,) + x.shape)

    share = jnp.sum(trade(half, plane, ("x", "gy")), axis=0)
    share = jnp.sum(trade(copies(share, depth), depth, ("zh", "zl")), axis=0)
    whole = trade(copies(share, plane), plane, ("x", "gy"))
    whole = whole.reshape(PAY // 2, LANES)
    rest = lax.ppermute(whole, "core", swap)

    kernel_grad, bias_grad = pl.pallas_call(
        unpack_kernel,
        out_shape=(sds((27, channels, channels)), sds((1, channels))),
        in_specs=[SM, VM, VM],
        out_specs=(VM,) * 2,
        scratch_shapes=[pltpu.VMEM((PAY, LANES), F32)],
        name="unpack", compiler_params=ROOM,
    )(core, local(whole), local(rest))
    return input_grad, kernel_grad, bias_grad.reshape(channels)


def solution(mesh):
    shape = mesh.devices.shape
    fine = Mesh(mesh.devices.reshape(2, shape[0] // 2, shape[1], shape[2] // 2, 2), AX)
    placed = (
        P(AX, None, None),
        P(AX, None, None),
        P(AX, None, None),
        P(),
        P(AX, None),
        P(AX, None),
        P(AX, None),
        P(AX),
    )
    return jax.shard_map(
        shards,
        mesh=fine,
        in_specs=placed,
        out_specs=(P(AX, None, None), P(), P()),
        check_vma=False,
    )
```

```python
import functools

import jax
import jax.numpy as jnp
import numpy as np
from jax import lax
from jax.experimental import pallas as pl
from jax.experimental.pallas import tpu as pltpu
from jax.sharding import Mesh, PartitionSpec as P

F32 = jnp.float32
BF16 = jnp.bfloat16
BS = 8
VOL = 512
LANES = 128
PAY = 896
AX = "d"

FACE = 64


def layout_of(blocks, listed):
    face = listed * FACE
    edge = listed * BS
    corner = -(-listed // 8) * 8
    y_rows = face + 2 * edge
    z_rows = face + 4 * edge + 4 * corner
    starts = [0]
    for size in (face, face, y_rows, y_rows, z_rows):
        starts.append(starts[-1] + size)
    total = starts[-1] + z_rows
    return dict(face=face, edge=edge, corner=corner, y_rows=y_rows, z_rows=z_rows,
                starts=starts, total=total)


def log2(n):
    return int(n).bit_length() - 1


def piece_table(blocks, listed):
    lay = layout_of(blocks, listed)
    face, edge, corner, starts = lay["face"], lay["edge"], lay["corner"], lay["starts"]
    table = np.zeros((27, 28), np.int32)
    for o in range(27):
        off = (o // 9 - 1, o // 3 % 3 - 1, o % 3 - 1)
        if off == (0, 0, 0):
            continue
        fixed = [7 if v == -1 else 0 for v in off]
        axis = 0 if off[0] else (1 if off[1] else 2)
        plane = [i for i in range(3) if i != axis]
        for d in range(27):
            own = (d // 9 - 1, d // 3 % 3 - 1, d % 3 - 1)
            if any(v != 0 and v != w for v, w in zip(own, off)):
                continue
            side = [(v + 1) // 2 for v in own]
            if own == (0, 0, 0):
                base, mult, strides = 0, VOL, {0: 64, 1: 8, 2: 1}
            elif own[2]:
                base = starts[4 + side[2]]
                if own[0] and own[1]:
                    base += face + 4 * edge + corner * (side[1] * 2 + side[0])
                    mult, strides = 1, {}
                elif own[0]:
                    base += face + edge * side[0]
                    mult, strides = 8, {1: 1}
                elif own[1]:
                    base += face + 2 * edge + edge * side[1]
                    mult, strides = 8, {0: 1}
                else:
                    mult, strides = 64, {0: 8, 1: 1}
            elif own[1]:
                base = starts[2 + side[1]]
                if own[0]:
                    base += face + edge * side[0]
                    mult, strides = 8, {2: 1}
                else:
                    mult, strides = 64, {0: 8, 2: 1}
            else:
                base = starts[side[0]]
                mult, strides = 64, {1: 8, 2: 1}
            for i in range(3):
                if off[i] != 0:
                    base += fixed[i] * strides.get(i, 0)
            s1 = strides[plane[0]] if off[plane[0]] == 0 else 1
            s2 = strides[plane[1]] if off[plane[1]] == 0 else 1
            table[o, d] = base | log2(mult) << 12 | log2(s1) << 16 | log2(s2) << 20
    return table.reshape(-1)


def split_hl(value, mask):
    high = value.astype(BF16).astype(F32)
    return jnp.where(mask, high, value - high)


def pack_rows(ref, out):
    n = out.shape[0]
    left = lax.broadcasted_iota(jnp.int32, (n, LANES), 1) < 64
    out[...] = jnp.where(left, ref[0:n, :], ref[n : 2 * n, :])


def unpack_rows(ref, out, start=0):
    n = ref.shape[0]
    left = lax.broadcasted_iota(jnp.int32, (n, LANES), 1) < 64
    v = ref[...]
    w = pltpu.roll(v, 64, 1)
    out[start : start + n, :] = jnp.where(left, v, w)
    out[start + n : start + 2 * n, :] = jnp.where(left, w, v)


def prep_kernel(core, send_h, cot_h, pre_h, act_h, gd, xs0, xs1, ys, zs, send, cot, pre, act, sems, asem, ssem, xf):
    blocks = cot.shape[0]
    listed = send.shape[0]
    pairs = ((cot_h, cot, 0), (pre_h, pre, 1))
    copies = [[pltpu.make_async_copy(h.at[b], v.at[b], sems.at[b, i]) for h, v, i in pairs] for b in range(blocks)]
    act_copy = pltpu.make_async_copy(act_h, act, asem)
    send_copy = pltpu.make_async_copy(send_h, send, ssem)
    act_copy.start()
    for pair in copies:
        for copy in pair:
            copy.start()
    send_copy.start()
    act_copy.wait()
    for b in range(blocks):
        for copy in copies[b]:
            copy.wait()
        p = pre[b]
        s = 1.0 / (1.0 + jnp.exp(-p))
        m = act[b : b + 1, :].astype(F32)
        g = cot[b] * (s * (1.0 + p * (1.0 - s))) * m
        gd[b * VOL : (b + 1) * VOL, :] = jnp.concatenate([g, g], axis=0).T
    send_copy.wait()
    for i in range(listed):
        r0 = pl.multiple_of(jnp.minimum(send[i], blocks - 1) * VOL, VOL)
        for side in range(2):
            f = 7 * side
            xf[side, i * 64 : (i + 1) * 64, :] = gd[pl.ds(r0 + f * 64, 64), :]
            for x in range(8):
                ys[side, i * 64 + x * 8 : i * 64 + x * 8 + 8, :] = gd[pl.ds(r0 + x * 64 + f * 8, 8), :]
            zs[side, i * 64 : (i + 1) * 64, :] = gd[pl.ds(r0 + f, 64, stride=8), :]
    pack_rows(xf.at[0], xs0)
    pack_rows(xf.at[1], xs1)


def pack_y_kernel(ys, rx0, rx1, after, out0, out1, xf, yf):
    face = ys.shape[1]
    listed = face // 64
    unpack_rows(rx0, xf.at[0])
    unpack_rows(rx1, xf.at[1])
    for side, out in ((0, out0), (1, out1)):
        f = 7 * side
        yf[0:face, :] = ys[side]
        for j in range(2):
            for s in range(listed):
                row = face + (j * listed + s) * 8
                yf[row : row + 8, :] = xf[j, s * 64 + f * 8 : s * 64 + f * 8 + 8, :]
        pack_rows(yf, out)


def pack_z_kernel(zs, rx0, rx1, ry0, ry1, after, out0, out1, x0, x1, y0, y1, zf):
    face = zs.shape[1]
    listed = face // 64
    edge = listed * 8
    corner = -(-listed // 8) * 8
    for src, full in ((rx0, x0), (rx1, x1), (ry0, y0), (ry1, y1)):
        unpack_rows(src, full)
    for side, out in ((0, out0), (1, out1)):
        f = 7 * side
        zf[0:face, :] = zs[side]
        for j, src in enumerate((x0, x1, y0, y1)):
            row = face + j * edge
            zf[row : row + edge, :] = src[pl.ds(f, edge, stride=8), :]
        for j, src in enumerate((y0, y1)):
            for i in range(2):
                row = face + 4 * edge + corner * (2 * j + i)
                zf[row : row + corner, :] = jnp.zeros((corner, LANES), F32)
                for s in range(listed):
                    at = face + i * edge + s * 8 + f
                    zf[row + s : row + s + 1, :] = src[at : at + 1, :]
        pack_rows(zf, out)


def interior_block(b, r0, gd, feat, act, at, p, kg_in, kg, rt, bias_in, bias, z):
    lane = lax.broadcasted_iota(jnp.int32, (VOL, LANES), 1) < 64
    rows = slice(r0, r0 + VOL)
    g = gd[b * VOL : (b + 1) * VOL, :]
    total = jnp.broadcast_to(jnp.sum(g, axis=0, keepdims=True), bias.shape)
    bias[...] = total if bias_in is None else bias_in[...] + total
    hl = split_hl(g, lane)
    row = lax.broadcasted_iota(jnp.int32, (VOL, LANES), 0)
    vy = (row // 8) % 8
    vz = row % 8
    for kz in (-1, 0, 1):
        if kz == 0:
            sz = hl
        elif kz == 1:
            sz = jnp.where(vz >= 1, pltpu.roll(hl, 1, 0), 0.0)
        else:
            sz = jnp.where(vz <= 6, pltpu.roll(hl, VOL - 1, 0), 0.0)
        for ky in (-1, 0, 1):
            if ky == 0:
                sy = sz
            elif ky == 1:
                sy = jnp.where(vy >= 1, pltpu.roll(sz, 8, 0), 0.0)
            else:
                sy = jnp.where(vy <= 6, pltpu.roll(sz, VOL - 8, 0), 0.0)
            c = (ky + 1) * 3 + kz + 1
            z[:, c * 128 : (c + 1) * 128] = sy.astype(BF16)

    f = feat * act[b : b + 1, :].astype(F32)
    ff = jnp.concatenate([f, f], axis=0)
    half = lax.broadcasted_iota(jnp.int32, (LANES, VOL), 0) < 64
    a = split_hl(ff, half)
    at[rows, :] = a.T
    zero = jnp.zeros((LANES, 64), F32)
    up = jnp.concatenate([zero, a[:, : VOL - 64]], axis=1)
    down = jnp.concatenate([a[:, 64:], zero], axis=1)
    a3 = jnp.concatenate([up, a, down], axis=0).astype(BF16)
    term = jnp.dot(a3, z[...], preferred_element_type=F32)
    kg[...] = term if kg_in is None else kg_in[...] + term
    p3 = lax.dot_general(z[...], rt[...], (((1,), (1,)), ((), ())), preferred_element_type=F32)
    p[rows, :] = p3[:, 128:256]
    p[r0 + 64 : r0 + VOL, :] += p3[: VOL - 64, 256:384]
    p[r0 : r0 + VOL - 64, :] += p3[64:, 0:128]


def fetch(part, feat_h, feat, sems):
    return [pltpu.make_async_copy(feat_h.at[b], feat.at[i], sems.at[i]) for i, b in enumerate(part)]


def first_kernel(part, gd, feat_h, act, kern_h, at, p, kg, rt, bias, z, feat, sems, kern, ksem):
    kern_copy = pltpu.make_async_copy(kern_h, kern, ksem)
    kern_copy.start()
    copies = fetch(part, feat_h, feat, sems)
    for copy in copies:
        copy.start()
    kern_copy.wait()
    for k in range(27):
        kx, c = k // 9, k % 9
        w = kern[k]
        wd = jnp.concatenate([w, w], axis=1)
        high = wd.astype(BF16)
        low = (wd - high.astype(F32)).astype(BF16)
        rt[kx * 128 : kx * 128 + 64, c * 128 : (c + 1) * 128] = high
        rt[kx * 128 + 64 : kx * 128 + 128, c * 128 : (c + 1) * 128] = low
    for i, b in enumerate(part):
        copies[i].wait()
        kgi, bi = (None, None) if i == 0 else (kg, bias)
        interior_block(b, i * VOL, gd, feat[i], act, at, p, kgi, kg, rt, bi, bias, z)


def next_kernel(part, held, *refs):
    gd, feat_h, act, rt, kg0, bias0 = refs[:6]
    earlier = refs[6 : 6 + 2 * held]
    at, p, kg, bias, z, feat, sems = refs[7 + 2 * held :]
    copies = fetch(part, feat_h, feat, sems)
    for copy in copies:
        copy.start()
    row = 0
    for i in range(held):
        n = earlier[2 * i].shape[0]
        at[row : row + n, :] = earlier[2 * i][...]
        p[row : row + n, :] = earlier[2 * i + 1][...]
        row += n
    for i, b in enumerate(part):
        copies[i].wait()
        kgi, bi = (kg0, bias0) if i == 0 else (kg, bias)
        interior_block(b, row + i * VOL, gd, feat[i], act, at, p, kgi, kg, rt, bi, bias, z)


def nt(a, b):
    return lax.dot_general(a, b, (((1,), (1,)), ((), ())), preferred_element_type=F32)


def tn(a, b):
    return lax.dot_general(a, b, (((0,), (0,)), ((), ())), preferred_element_type=F32)


def plane_pieces(axis, sign):
    out = []
    for o in range(27):
        off = (o // 9 - 1, o // 3 % 3 - 1, o % 3 - 1)
        if off[axis] == sign and all(off[i] == 0 for i in range(axis)):
            r, q = [off[i] for i in range(3) if i != axis]
            out.append((o, r, q))
    return out


def plane_slot(b, axis, sign):
    return b * 6 + 2 * axis + (sign + 1) // 2


def for_planes(od, visit):
    def block(b, carry):
        for axis in range(3):
            for sign in (-1, 1):
                pieces = plane_pieces(axis, sign)
                found = od[b, pieces[0][0]] != 27
                for o, _, _ in pieces[1:]:
                    found = found | (od[b, o] != 27)

                @pl.when(found)
                def _(axis=axis, sign=sign):
                    visit(b, axis, sign)

        return carry

    lax.fori_loop(0, od.shape[0], block, 0)


def edges_kernel(od, pws, rt, p, pa):
    pa[...] = p[...]

    def plane(b, axis, sign):
        face = 0 if sign == -1 else 7
        pw = pws.at[plane_slot(b, axis, sign)]
        r0 = b * VOL
        k = 1 - sign
        if axis == 0:
            rows = pl.ds(pl.multiple_of(r0 + face * 64, 64), 64)
            pa[rows, :] += nt(pw[...], rt[k * 128 : (k + 1) * 128, :])
        elif axis == 1:
            acc = jnp.zeros((64, LANES), F32)
            for i in range(3):
                acc = acc + nt(pw[:, i * 384 : (i + 1) * 384], rt[i * 128 : (i + 1) * 128, k * 384 : (k + 1) * 384])
            for x in range(8):
                rows = pl.ds(pl.multiple_of(r0 + x * 64 + face * 8, 8), 8)
                pa[rows, :] += acc[x * 8 : x * 8 + 8, :]
        else:
            acc = jnp.zeros((64, LANES), F32)
            for i in range(3):
                for j in range(3):
                    part = pw[:, (i * 3 + j) * 128 : (i * 3 + j + 1) * 128]
                    acc = acc + nt(part, rt[i * 128 : (i + 1) * 128, (j * 3 + k) * 128 : (j * 3 + k + 1) * 128])
            rows = pl.ds(r0 + face, 64, stride=8)
            pa[rows, :] = pa[rows, :] + acc

    for_planes(od, plane)


def join_kernel(mine, arrived, after, half):
    half[...] = mine[...] + arrived[...]


def halo_kernel(scale, od, os_, tb, core, gd, rx0, rx1, ry0, ry1, rz0, rz1, at, bias, kg0,
                mine, other, pws, src, pb, pay, kg):
    blocks = od.shape[0]
    row = 0
    for ref in (rx0, rx1, ry0, ry1, rz0, rz1):
        unpack_rows(ref, src, row)
        row += 2 * ref.shape[0]
    kg[...] = kg0[...]
    lane64 = lax.broadcasted_iota(jnp.int32, (64, LANES), 1) < 64

    def plane(b, axis, sign):
        face = 0 if sign == -1 else 7
        pw = pws.at[plane_slot(b, axis, sign)]
        pb[...] = jnp.zeros(pb.shape, F32)
        for o, r, q in plane_pieces(axis, sign):
            d = od[b, o]

            @pl.when(d != 27)
            def _(o=o, r=r, q=q, d=d):
                code = tb[o * 28 + d]
                base = (code & 4095) + (os_[b, o] << ((code >> 12) & 15))
                sr = (code >> 16) & 15
                sq = (code >> 20) & 15

                def fill(ref):
                    for i in range(8 if r == 0 else 1):
                        for j in range(8 if q == 0 else 1):
                            at_r = i + 1 if r == 0 else (0 if r == -1 else 9)
                            at_q = 8 + j if q == 0 else (7 if q == -1 else 16)
                            row = base + (i << sr) + (j << sq)
                            pb[at_r, at_q : at_q + 1, :] = ref[pl.ds(row, 1), :]

                pl.when(d == 13)(lambda: fill(gd))
                pl.when(d != 13)(lambda: fill(src))

        for kr in (-1, 0, 1):
            for kq in (-1, 0, 1):
                win = pb[1 - kr : 9 - kr, 8 - kq : 16 - kq, :].reshape(64, LANES)
                c = (kr + 1) * 3 + kq + 1
                pw[:, c * 128 : (c + 1) * 128] = split_hl(win, lane64).astype(BF16)
        r0 = b * VOL
        k = 1 - sign
        if axis == 0:
            ap = at[pl.ds(pl.multiple_of(r0 + face * 64, 64), 64), :].astype(BF16)
            kg[k * 128 : (k + 1) * 128, :] += tn(ap, pw[...])
        elif axis == 1:
            starts = [pl.multiple_of(r0 + x * 64 + face * 8, 8) for x in range(8)]
            ap = jnp.concatenate([at[pl.ds(s, 8), :] for s in starts], axis=0).astype(BF16)
            for i in range(3):
                kg[i * 128 : (i + 1) * 128, k * 384 : (k + 1) * 384] += tn(ap, pw[:, i * 384 : (i + 1) * 384])
        else:
            ap = at[pl.ds(r0 + face, 64, stride=8), :].astype(BF16)
            for i in range(3):
                for j in range(3):
                    part = pw[:, (i * 3 + j) * 128 : (i * 3 + j + 1) * 128]
                    kg[i * 128 : (i + 1) * 128, (j * 3 + k) * 128 : (j * 3 + k + 1) * 128] += tn(ap, part)

    for_planes(od, plane)

    for n in range(28):
        t, odd = n // 2, n % 2
        if n < 27:
            kx, c = n // 9, n % 9
            lo, hi = c * 128, (c + 1) * 128
            u = kg[kx * 128 : kx * 128 + 64, lo:hi] + kg[kx * 128 + 64 : kx * 128 + 128, lo:hi]
            u = u + pltpu.roll(u, 64, 1)
        else:
            first = lax.broadcasted_iota(jnp.int32, (64, LANES), 0) == 0
            u = jnp.where(first, jnp.broadcast_to(bias[0:1, :], (64, LANES)), 0.0)
        if odd:
            pay[t * 64 : (t + 1) * 64, :] = jnp.where(lane64, held, u) * scale
        held = u
    me = core[0]
    mine[...] = pay[pl.ds(pl.multiple_of(me * (PAY // 2), PAY // 2), PAY // 2), :]
    other[...] = pay[pl.ds(pl.multiple_of((1 - me) * (PAY // 2), PAY // 2), PAY // 2), :]


def finish_kernel(pa, act, ig):
    for b in range(act.shape[0]):
        og = pa[b * VOL : (b + 1) * VOL, :]
        og = (og + pltpu.roll(og, 64, 1)).T
        ig[b] = og[:64, :] * act[b : b + 1, :].astype(F32)


def unpack_kernel(core, mine, other, kout, bout, pay):
    me = core[0]
    pay[pl.ds(pl.multiple_of(me * (PAY // 2), PAY // 2), PAY // 2), :] = mine[...]
    pay[pl.ds(pl.multiple_of((1 - me) * (PAY // 2), PAY // 2), PAY // 2), :] = other[...]
    for t in range(14):
        tile = pay[t * 64 : (t + 1) * 64, :]
        turned = pltpu.roll(tile, 64, 1)
        kout[2 * t] = tile[:, :64]
        if t < 13:
            kout[2 * t + 1] = turned[:, :64]
        else:
            bout[...] = turned[0:1, :64]


VM = pl.BlockSpec(memory_space=pltpu.VMEM)
SM = pl.BlockSpec(memory_space=pltpu.SMEM)
ANY = pl.BlockSpec(memory_space=pl.ANY)
ROOM = pltpu.CompilerParams(vmem_limit_bytes=32 * 2**20)


def sds(shape, dtype=F32):
    return jax.ShapeDtypeStruct(shape, dtype)


def both_ways(low, high, ids, axis):
    lines = np.moveaxis(ids, axis, -1)
    steps = [(int(a), int(b)) for a, b in zip(lines[..., :-1].ravel(), lines[..., 1:].ravel())]
    up = lax.ppermute(high, AX, steps)
    down = lax.ppermute(low, AX, [(b, a) for a, b in steps])
    return up, down


def sum_groups(ids):
    zh, x, y, zl, _ = ids.shape
    first, second = [], []
    for core in range(2):
        part = ids[..., core]
        if core == 0 or y != zh * zl:
            first += part.transpose(0, 3, 1, 2).reshape(zh * zl, x * y).tolist()
            second += part.transpose(1, 2, 0, 3).reshape(x * y, zh * zl).tolist()
        else:
            first += part.transpose(2, 1, 0, 3).reshape(y, x * zh * zl).tolist()
            second += part.transpose(1, 0, 3, 2).reshape(x * zh * zl, y).tolist()
    return first, second


def vm(shape, dtype=F32):
    return pltpu.VMEM(shape, dtype)


def local(x):
    return pltpu.with_memory_space_constraint(x, pltpu.VMEM)


def far(x):
    return pltpu.with_memory_space_constraint(x, pltpu.HBM)


def shards(grid, features, preact, cotangent, kernel, active, owner_dir, owner_slot, send_list):
    blocks, channels, volume = features.shape
    listed = send_list.shape[0]
    lay = layout_of(blocks, listed)
    face, yr, zr = lay["face"], lay["y_rows"], lay["z_rows"]
    rows = blocks * VOL
    devices = int(np.prod(grid))
    ids = np.arange(devices).reshape(grid)
    core = (lax.axis_index(AX) & 1).astype(jnp.int32).reshape(1)
    scale = float((volume * blocks * devices) ** -0.5)

    gd, xs0, xs1, ys, zs = pl.pallas_call(
        prep_kernel,
        out_shape=(vm((rows, LANES)), vm((face // 2, LANES)), vm((face // 2, LANES)), vm((2, face, LANES)), vm((2, face, LANES))),
        in_specs=[SM] + [ANY] * 4,
        out_specs=(VM,) * 5,
        scratch_shapes=[
            pltpu.SMEM((listed,), jnp.int32),
            pltpu.VMEM((blocks, channels, VOL), F32),
            pltpu.VMEM((blocks, channels, VOL), F32),
            pltpu.VMEM((blocks, VOL), jnp.int32),
            pltpu.SemaphoreType.DMA((blocks, 2)),
            pltpu.SemaphoreType.DMA,
            pltpu.SemaphoreType.DMA,
            pltpu.VMEM((2, face, LANES), F32),
        ],
        name="prep", compiler_params=ROOM,
    )(core, far(send_list), far(cotangent), far(preact), far(active))
    rx0, rx1 = both_ways(xs0, xs1, ids, 0)

    third = max(blocks // 4, 1)
    parts = (range(third), range(third, 2 * third), range(2 * third, blocks))

    def scratch(part):
        return [
            pltpu.VMEM((VOL, 1152), BF16),
            pltpu.VMEM((max(len(part), 1), channels, VOL), F32),
            pltpu.SemaphoreType.DMA((max(len(part), 1),)),
        ]

    wide = (384, 1152)
    n0 = len(parts[0]) * VOL
    at0, p0, kg, rt, bias = pl.pallas_call(
        functools.partial(first_kernel, parts[0]),
        in_specs=[VM, ANY, VM, ANY],
        out_specs=(VM,) * 5,
        out_shape=(vm((n0, LANES)), vm((n0, LANES)), vm(wide), vm(wide, BF16), vm((8, LANES))),
        scratch_shapes=scratch(parts[0]) + [pltpu.VMEM((27, channels, channels), F32), pltpu.SemaphoreType.DMA],
        name="interior0", compiler_params=ROOM,
    )(local(gd), far(features), active, far(kernel))

    def more(part, earlier, kg, bias, after, name):
        n = len(part) * VOL + sum(e.shape[0] for e in earlier[::2])
        return pl.pallas_call(
            functools.partial(next_kernel, part, len(earlier) // 2),
            in_specs=[VM, ANY] + [VM] * (4 + len(earlier)) + [ANY],
            out_specs=(VM,) * 4,
            out_shape=(vm((n, LANES)), vm((n, LANES)), vm(wide), vm((8, LANES))),
            scratch_shapes=scratch(part),
            name=name, compiler_params=ROOM,
        )(local(gd), far(features), active, local(rt), local(kg), local(bias), *[local(e) for e in earlier], after)

    ys0, ys1 = pl.pallas_call(
        pack_y_kernel, out_shape=(vm((yr // 2, LANES)),) * 2,
        scratch_shapes=[pltpu.VMEM((2, face, LANES), F32), pltpu.VMEM((yr, LANES), F32)],
        in_specs=[VM] * 3 + [ANY], out_specs=(VM,) * 2,
        name="pack_y", compiler_params=ROOM,
    )(local(ys), local(rx0), local(rx1), bias)
    ry0, ry1 = both_ways(ys0, ys1, ids, 1)
    at1, p1, kg, bias = more(parts[1], (), kg, bias, ys0, "interior1")
    zs0, zs1 = pl.pallas_call(
        pack_z_kernel, out_shape=(vm((zr // 2, LANES)),) * 2,
        scratch_shapes=[pltpu.VMEM((n, LANES), F32) for n in (face, face, yr, yr, zr)],
        in_specs=[VM] * 5 + [ANY], out_specs=(VM,) * 2,
        name="pack_z", compiler_params=ROOM,
    )(local(zs), local(rx0), local(rx1), local(ry0), local(ry1), bias)
    rz0, rz1 = both_ways(zs0, zs1, ids, 2)
    at, p, kg, bias = more(parts[2], (at0, p0, at1, p1), kg, bias, zs0, "interior2")

    table = jnp.asarray(piece_table(blocks, listed))
    mine, other, pws = pl.pallas_call(
        functools.partial(halo_kernel, scale),
        out_shape=(vm((PAY // 2, LANES)), vm((PAY // 2, LANES)), vm((6 * blocks, 64, 1152), BF16)),
        in_specs=[SM] * 4 + [VM] * 10,
        out_specs=(VM,) * 3,
        scratch_shapes=[
            pltpu.VMEM((lay["total"], LANES), F32),
            pltpu.VMEM((10, 24, LANES), F32),
            pltpu.VMEM((PAY, LANES), F32),
            pltpu.VMEM((384, 1152), F32),
        ],
        name="halo", compiler_params=ROOM,
    )(owner_dir, owner_slot, table, core, local(gd), local(rx0), local(rx1), local(ry0), local(ry1),
      local(rz0), local(rz1), local(at), local(bias), local(kg))

    swap = [(i, i ^ 1) for i in range(devices)]
    arrived = lax.ppermute(other, AX, swap)
    p = pl.pallas_call(
        edges_kernel, out_shape=vm((rows, LANES)), in_specs=[SM] + [VM] * 3, out_specs=VM,
        name="edges", compiler_params=ROOM,
    )(owner_dir, local(pws), local(rt), local(p))
    half = pl.pallas_call(
        join_kernel, out_shape=vm((PAY // 2, LANES)), in_specs=[VM, VM, ANY], out_specs=VM,
        name="join", compiler_params=ROOM,
    )(local(mine), local(arrived), p)
    over, along = sum_groups(ids.reshape(2, grid[0] // 2, grid[1], grid[2] // 2, 2))
    plane, depth = len(over[0]), len(along[0])
    chunk = PAY // 2 // plane // 2

    def trade(x, groups):
        x = x.reshape(len(groups[0]) * chunk, 2, LANES)
        x = lax.all_to_all(x, AX, 0, 0, tiled=True, axis_index_groups=groups)
        return x.reshape(len(groups[0]), chunk, 2, LANES)

    def copies(x, count):
        return jnp.broadcast_to(x[None], (count,) + x.shape)

    share = jnp.sum(trade(half, over), axis=0)
    share = jnp.sum(trade(copies(share, depth), along), axis=0)
    whole = trade(copies(share, plane), over)
    whole = whole.reshape(PAY // 2, LANES)
    rest = lax.ppermute(whole, AX, swap)
    input_grad = pl.pallas_call(
        finish_kernel, out_shape=sds((blocks, channels, VOL)), in_specs=[VM] * 2, out_specs=VM,
        name="finish", compiler_params=ROOM,
    )(local(p), active)

    kernel_grad, bias_grad = pl.pallas_call(
        unpack_kernel,
        out_shape=(sds((27, channels, channels)), sds((1, channels))),
        in_specs=[SM, VM, VM],
        out_specs=(VM,) * 2,
        scratch_shapes=[pltpu.VMEM((PAY, LANES), F32)],
        name="unpack", compiler_params=ROOM,
    )(core, local(whole), local(rest))
    return input_grad, kernel_grad, bias_grad.reshape(channels)


def solution(mesh):
    grid = mesh.devices.shape
    flat = Mesh(mesh.devices.reshape(-1), (AX,))
    placed = (
        P(AX, None, None),
        P(AX, None, None),
        P(AX, None, None),
        P(),
        P(AX, None),
        P(AX, None),
        P(AX, None),
        P(AX),
    )
    return jax.shard_map(
        functools.partial(shards, grid),
        mesh=flat,
        in_specs=placed,
        out_specs=(P(AX, None, None), P(), P()),
        check_vma=False,
    )
```

```python
import functools

import jax
import jax.numpy as jnp
import numpy as np
from jax import lax
from jax.experimental import pallas as pl
from jax.experimental.pallas import tpu as pltpu
from jax.sharding import Mesh, PartitionSpec as P

F32 = jnp.float32
BF16 = jnp.bfloat16
BS = 8
VOL = 512
LANES = 128
PAY = 896
AX = "d"

FACE = 64


def layout_of(blocks, listed):
    face = listed * FACE
    edge = listed * BS
    corner = -(-listed // 8) * 8
    y_rows = face + 2 * edge
    z_rows = face + 4 * edge + 4 * corner
    starts = [0]
    for size in (face, face, y_rows, y_rows, z_rows):
        starts.append(starts[-1] + size)
    total = starts[-1] + z_rows
    return dict(face=face, edge=edge, corner=corner, y_rows=y_rows, z_rows=z_rows,
                starts=starts, total=total)


def log2(n):
    return int(n).bit_length() - 1


def piece_table(blocks, listed):
    lay = layout_of(blocks, listed)
    face, edge, corner, starts = lay["face"], lay["edge"], lay["corner"], lay["starts"]
    table = np.zeros((27, 28), np.int32)
    for o in range(27):
        off = (o // 9 - 1, o // 3 % 3 - 1, o % 3 - 1)
        if off == (0, 0, 0):
            continue
        fixed = [7 if v == -1 else 0 for v in off]
        axis = 0 if off[0] else (1 if off[1] else 2)
        plane = [i for i in range(3) if i != axis]
        for d in range(27):
            own = (d // 9 - 1, d // 3 % 3 - 1, d % 3 - 1)
            if any(v != 0 and v != w for v, w in zip(own, off)):
                continue
            side = [(v + 1) // 2 for v in own]
            if own == (0, 0, 0):
                base, mult, strides = 0, VOL, {0: 64, 1: 8, 2: 1}
            elif own[2]:
                base = starts[4 + side[2]]
                if own[0] and own[1]:
                    base += face + 4 * edge + corner * (side[1] * 2 + side[0])
                    mult, strides = 1, {}
                elif own[0]:
                    base += face + edge * side[0]
                    mult, strides = 8, {1: 1}
                elif own[1]:
                    base += face + 2 * edge + edge * side[1]
                    mult, strides = 8, {0: 1}
                else:
                    mult, strides = 64, {0: 8, 1: 1}
            elif own[1]:
                base = starts[2 + side[1]]
                if own[0]:
                    base += face + edge * side[0]
                    mult, strides = 8, {2: 1}
                else:
                    mult, strides = 64, {0: 8, 2: 1}
            else:
                base = starts[side[0]]
                mult, strides = 64, {1: 8, 2: 1}
            for i in range(3):
                if off[i] != 0:
                    base += fixed[i] * strides.get(i, 0)
            s1 = strides[plane[0]] if off[plane[0]] == 0 else 1
            s2 = strides[plane[1]] if off[plane[1]] == 0 else 1
            table[o, d] = base | log2(mult) << 12 | log2(s1) << 16 | log2(s2) << 20
    return table.reshape(-1)


def split_hl(value, mask):
    high = value.astype(BF16).astype(F32)
    return jnp.where(mask, high, value - high)


def pack_rows(ref, out):
    n = out.shape[0]
    left = lax.broadcasted_iota(jnp.int32, (n, LANES), 1) < 64
    out[...] = jnp.where(left, ref[0:n, :], ref[n : 2 * n, :])


def unpack_rows(ref, out, start=0):
    n = ref.shape[0]
    left = lax.broadcasted_iota(jnp.int32, (n, LANES), 1) < 64
    v = ref[...]
    w = pltpu.roll(v, 64, 1)
    out[start : start + n, :] = jnp.where(left, v, w)
    out[start + n : start + 2 * n, :] = jnp.where(left, w, v)


def prep_kernel(core, send_h, cot_h, pre_h, act_h, gd, xs0, xs1, ys, zs, send, cot, pre, act, sems, asem, ssem, xf):
    blocks = cot.shape[0]
    listed = send.shape[0]
    pairs = ((cot_h, cot, 0), (pre_h, pre, 1))
    copies = [[pltpu.make_async_copy(h.at[b], v.at[b], sems.at[b, i]) for h, v, i in pairs] for b in range(blocks)]
    act_copy = pltpu.make_async_copy(act_h, act, asem)
    send_copy = pltpu.make_async_copy(send_h, send, ssem)
    act_copy.start()
    for pair in copies:
        for copy in pair:
            copy.start()
    send_copy.start()
    act_copy.wait()
    for b in range(blocks):
        for copy in copies[b]:
            copy.wait()
        p = pre[b]
        s = 1.0 / (1.0 + jnp.exp(-p))
        m = act[b : b + 1, :].astype(F32)
        g = cot[b] * (s * (1.0 + p * (1.0 - s))) * m
        gd[b * VOL : (b + 1) * VOL, :] = jnp.concatenate([g, g], axis=0).T
    send_copy.wait()
    for i in range(listed):
        r0 = pl.multiple_of(jnp.minimum(send[i], blocks - 1) * VOL, VOL)
        for side in range(2):
            f = 7 * side
            xf[side, i * 64 : (i + 1) * 64, :] = gd[pl.ds(r0 + f * 64, 64), :]
            for x in range(8):
                ys[side, i * 64 + x * 8 : i * 64 + x * 8 + 8, :] = gd[pl.ds(r0 + x * 64 + f * 8, 8), :]
            zs[side, i * 64 : (i + 1) * 64, :] = gd[pl.ds(r0 + f, 64, stride=8), :]
    pack_rows(xf.at[0], xs0)
    pack_rows(xf.at[1], xs1)


def pack_y_kernel(ys, rx0, rx1, after, out0, out1, xf, yf):
    face = ys.shape[1]
    listed = face // 64
    unpack_rows(rx0, xf.at[0])
    unpack_rows(rx1, xf.at[1])
    for side, out in ((0, out0), (1, out1)):
        f = 7 * side
        yf[0:face, :] = ys[side]
        for j in range(2):
            for s in range(listed):
                row = face + (j * listed + s) * 8
                yf[row : row + 8, :] = xf[j, s * 64 + f * 8 : s * 64 + f * 8 + 8, :]
        pack_rows(yf, out)


def pack_z_kernel(zs, rx0, rx1, ry0, ry1, after, out0, out1, x0, x1, y0, y1, zf):
    face = zs.shape[1]
    listed = face // 64
    edge = listed * 8
    corner = -(-listed // 8) * 8
    for src, full in ((rx0, x0), (rx1, x1), (ry0, y0), (ry1, y1)):
        unpack_rows(src, full)
    for side, out in ((0, out0), (1, out1)):
        f = 7 * side
        zf[0:face, :] = zs[side]
        for j, src in enumerate((x0, x1, y0, y1)):
            row = face + j * edge
            zf[row : row + edge, :] = src[pl.ds(f, edge, stride=8), :]
        for j, src in enumerate((y0, y1)):
            for i in range(2):
                row = face + 4 * edge + corner * (2 * j + i)
                zf[row : row + corner, :] = jnp.zeros((corner, LANES), F32)
                for s in range(listed):
                    at = face + i * edge + s * 8 + f
                    zf[row + s : row + s + 1, :] = src[at : at + 1, :]
        pack_rows(zf, out)


def interior_block(b, r0, gd, feat, act, at, p, kg_in, kg, rt, bias_in, bias, z):
    lane = lax.broadcasted_iota(jnp.int32, (VOL, LANES), 1) < 64
    rows = slice(r0, r0 + VOL)
    g = gd[b * VOL : (b + 1) * VOL, :]
    total = jnp.broadcast_to(jnp.sum(g, axis=0, keepdims=True), bias.shape)
    bias[...] = total if bias_in is None else bias_in[...] + total
    hl = split_hl(g, lane)
    row = lax.broadcasted_iota(jnp.int32, (VOL, LANES), 0)
    vy = (row // 8) % 8
    vz = row % 8
    for kz in (-1, 0, 1):
        if kz == 0:
            sz = hl
        elif kz == 1:
            sz = jnp.where(vz >= 1, pltpu.roll(hl, 1, 0), 0.0)
        else:
            sz = jnp.where(vz <= 6, pltpu.roll(hl, VOL - 1, 0), 0.0)
        for ky in (-1, 0, 1):
            if ky == 0:
                sy = sz
            elif ky == 1:
                sy = jnp.where(vy >= 1, pltpu.roll(sz, 8, 0), 0.0)
            else:
                sy = jnp.where(vy <= 6, pltpu.roll(sz, VOL - 8, 0), 0.0)
            c = (ky + 1) * 3 + kz + 1
            z[:, c * 128 : (c + 1) * 128] = sy.astype(BF16)

    f = feat * act[b : b + 1, :].astype(F32)
    ff = jnp.concatenate([f, f], axis=0)
    half = lax.broadcasted_iota(jnp.int32, (LANES, VOL), 0) < 64
    a = split_hl(ff, half)
    at[rows, :] = a.T
    zero = jnp.zeros((LANES, 64), F32)
    up = jnp.concatenate([zero, a[:, : VOL - 64]], axis=1)
    down = jnp.concatenate([a[:, 64:], zero], axis=1)
    a3 = jnp.concatenate([up, a, down], axis=0).astype(BF16)
    term = jnp.dot(a3, z[...], preferred_element_type=F32)
    kg[...] = term if kg_in is None else kg_in[...] + term
    p3 = lax.dot_general(z[...], rt[...], (((1,), (1,)), ((), ())), preferred_element_type=F32)
    p[rows, :] = p3[:, 128:256]
    p[r0 + 64 : r0 + VOL, :] += p3[: VOL - 64, 256:384]
    p[r0 : r0 + VOL - 64, :] += p3[64:, 0:128]


def fetch(part, feat_h, feat, sems):
    return [pltpu.make_async_copy(feat_h.at[b], feat.at[i], sems.at[i]) for i, b in enumerate(part)]


def first_kernel(part, gd, feat_h, act, kern_h, at, p, kg, rt, bias, z, feat, sems, kern, ksem):
    kern_copy = pltpu.make_async_copy(kern_h, kern, ksem)
    kern_copy.start()
    copies = fetch(part, feat_h, feat, sems)
    for copy in copies:
        copy.start()
    kern_copy.wait()
    for k in range(27):
        kx, c = k // 9, k % 9
        w = kern[k]
        wd = jnp.concatenate([w, w], axis=1)
        high = wd.astype(BF16)
        low = (wd - high.astype(F32)).astype(BF16)
        rt[kx * 128 : kx * 128 + 64, c * 128 : (c + 1) * 128] = high
        rt[kx * 128 + 64 : kx * 128 + 128, c * 128 : (c + 1) * 128] = low
    for i, b in enumerate(part):
        copies[i].wait()
        kgi, bi = (None, None) if i == 0 else (kg, bias)
        interior_block(b, i * VOL, gd, feat[i], act, at, p, kgi, kg, rt, bi, bias, z)


def plane_weights(rt, rtp):
    for i in range(3):
        rows = slice(i * 128, (i + 1) * 128)
        for s, k in enumerate((0, 2)):
            rtp[s, :, i * 384 : (i + 1) * 384] = rt[rows, k * 384 : (k + 1) * 384]
            for j in range(3):
                c = i * 3 + j
                rtp[2 + s, :, c * 128 : (c + 1) * 128] = rt[rows, (j * 3 + k) * 128 : (j * 3 + k + 1) * 128]


def next_kernel(part, held, *refs):
    gd, feat_h, act, rt, kg0, bias0 = refs[:6]
    earlier = refs[6 : 6 + 2 * held]
    at, p, kg, bias, rtp, z, feat, sems = refs[7 + 2 * held :]
    copies = fetch(part, feat_h, feat, sems)
    for copy in copies:
        copy.start()
    if held:
        rtp[...] = jnp.zeros(rtp.shape, rtp.dtype)
    else:
        plane_weights(rt, rtp)
    row = 0
    for i in range(held):
        n = earlier[2 * i].shape[0]
        at[row : row + n, :] = earlier[2 * i][...]
        p[row : row + n, :] = earlier[2 * i + 1][...]
        row += n
    for i, b in enumerate(part):
        copies[i].wait()
        kgi, bi = (kg0, bias0) if i == 0 else (kg, bias)
        interior_block(b, row + i * VOL, gd, feat[i], act, at, p, kgi, kg, rt, bi, bias, z)


def nt(a, b):
    return lax.dot_general(a, b, (((1,), (1,)), ((), ())), preferred_element_type=F32)


def tn(a, b):
    return lax.dot_general(a, b, (((0,), (0,)), ((), ())), preferred_element_type=F32)


def plane_pieces(axis, sign):
    out = []
    for o in range(27):
        off = (o // 9 - 1, o // 3 % 3 - 1, o % 3 - 1)
        if off[axis] == sign and all(off[i] == 0 for i in range(axis)):
            r, q = [off[i] for i in range(3) if i != axis]
            out.append((o, r, q))
    return out


def plane_slot(b, axis, sign):
    return b * 6 + 2 * axis + (sign + 1) // 2


def for_planes(od, visit):
    def block(b, carry):
        for axis in range(3):
            for sign in (-1, 1):
                pieces = plane_pieces(axis, sign)
                found = od[b, pieces[0][0]] != 27
                for o, _, _ in pieces[1:]:
                    found = found | (od[b, o] != 27)

                @pl.when(found)
                def _(axis=axis, sign=sign):
                    visit(b, axis, sign)

        return carry

    lax.fori_loop(0, od.shape[0], block, 0)


def edges_kernel(od, pws, rt, rtp, p, pa):
    pa[...] = p[...]

    def plane(b, axis, sign):
        face = 0 if sign == -1 else 7
        pw = pws[plane_slot(b, axis, sign)]
        r0 = b * VOL
        k = 1 - sign
        if axis == 0:
            rows = pl.ds(pl.multiple_of(r0 + face * 64, 64), 64)
            pa[rows, :] += nt(pw, rt[k * 128 : (k + 1) * 128, :])
        elif axis == 1:
            acc = nt(pw, rtp[k // 2])
            for x in range(8):
                rows = pl.ds(pl.multiple_of(r0 + x * 64 + face * 8, 8), 8)
                pa[rows, :] += acc[x * 8 : x * 8 + 8, :]
        else:
            rows = pl.ds(r0 + face, 64, stride=8)
            pa[rows, :] = pa[rows, :] + nt(pw, rtp[2 + k // 2])

    for_planes(od, plane)


def join_kernel(mine, arrived, after, half):
    half[...] = mine[...] + arrived[...]


def halo_kernel(scale, od, os_, tb, core, gd, rx0, rx1, ry0, ry1, rz0, rz1, at, bias, kg0,
                mine, other, pws, src, pb, pay, kg):
    blocks = od.shape[0]
    row = 0
    for ref in (rx0, rx1, ry0, ry1, rz0, rz1):
        unpack_rows(ref, src, row)
        row += 2 * ref.shape[0]
    kg[...] = kg0[...]
    lane64 = lax.broadcasted_iota(jnp.int32, (64, LANES), 1) < 64
    lane24 = lax.broadcasted_iota(jnp.int32, (10, 24, LANES), 2) < 64

    def plane(b, axis, sign):
        face = 0 if sign == -1 else 7
        pw = pws.at[plane_slot(b, axis, sign)]
        pb[...] = jnp.zeros(pb.shape, F32)
        for o, r, q in plane_pieces(axis, sign):
            d = od[b, o]

            @pl.when(d != 27)
            def _(o=o, r=r, q=q, d=d):
                code = tb[o * 28 + d]
                base = (code & 4095) + (os_[b, o] << ((code >> 12) & 15))
                sr = (code >> 16) & 15
                sq = (code >> 20) & 15

                def fill(ref, own):
                    if r == 0 and q == 0:
                        for i in range(8):
                            start = base + (i << sr)
                            if axis == 2 and own:
                                rows = pl.ds(start, 8, stride=8)
                            else:
                                rows = pl.ds(pl.multiple_of(start, 8), 8)
                            pb[i + 1, 8:16, :] = ref[rows, :]
                        return
                    for i in range(8 if r == 0 else 1):
                        for j in range(8 if q == 0 else 1):
                            at_r = i + 1 if r == 0 else (0 if r == -1 else 9)
                            at_q = 8 + j if q == 0 else (7 if q == -1 else 16)
                            row = base + (i << sr) + (j << sq)
                            pb[at_r, at_q : at_q + 1, :] = ref[pl.ds(row, 1), :]

                pl.when(d == 13)(lambda: fill(gd, True))
                pl.when(d != 13)(lambda: fill(src, False))

        pb[...] = split_hl(pb[...], lane24)
        for kr in (-1, 0, 1):
            for kq in (-1, 0, 1):
                win = pb[1 - kr : 9 - kr, 8 - kq : 16 - kq, :].reshape(64, LANES)
                c = (kr + 1) * 3 + kq + 1
                pw[:, c * 128 : (c + 1) * 128] = win.astype(BF16)
        r0 = b * VOL
        k = 1 - sign
        if axis == 0:
            ap = at[pl.ds(pl.multiple_of(r0 + face * 64, 64), 64), :]
        elif axis == 1:
            starts = [pl.multiple_of(r0 + x * 64 + face * 8, 8) for x in range(8)]
            ap = jnp.concatenate([at[pl.ds(s, 8), :] for s in starts], axis=0)
        else:
            ap = at[pl.ds(r0 + face, 64, stride=8), :]
        term = tn(ap.astype(BF16), pw[...])
        if axis == 0:
            kg[k * 128 : (k + 1) * 128, :] += term
        elif axis == 1:
            for i in range(3):
                kg[i * 128 : (i + 1) * 128, k * 384 : (k + 1) * 384] += term[:, i * 384 : (i + 1) * 384]
        else:
            for i in range(3):
                for j in range(3):
                    c = i * 3 + j
                    kg[i * 128 : (i + 1) * 128, (j * 3 + k) * 128 : (j * 3 + k + 1) * 128] += (
                        term[:, c * 128 : (c + 1) * 128]
                    )

    for_planes(od, plane)

    for n in range(28):
        t, odd = n // 2, n % 2
        if n < 27:
            kx, c = n // 9, n % 9
            lo, hi = c * 128, (c + 1) * 128
            u = kg[kx * 128 : kx * 128 + 64, lo:hi] + kg[kx * 128 + 64 : kx * 128 + 128, lo:hi]
            u = u + pltpu.roll(u, 64, 1)
        else:
            first = lax.broadcasted_iota(jnp.int32, (64, LANES), 0) == 0
            u = jnp.where(first, jnp.broadcast_to(bias[0:1, :], (64, LANES)), 0.0)
        if odd:
            pay[t * 64 : (t + 1) * 64, :] = jnp.where(lane64, held, u) * scale
        held = u
    me = core[0]
    mine[...] = pay[pl.ds(pl.multiple_of(me * (PAY // 2), PAY // 2), PAY // 2), :]
    other[...] = pay[pl.ds(pl.multiple_of((1 - me) * (PAY // 2), PAY // 2), PAY // 2), :]


def finish_kernel(pa, act, ig):
    for b in range(act.shape[0]):
        og = pa[b * VOL : (b + 1) * VOL, :]
        og = (og + pltpu.roll(og, 64, 1)).T
        ig[b] = og[:64, :] * act[b : b + 1, :].astype(F32)


def unpack_kernel(core, mine, other, kout, bout, pay):
    me = core[0]
    pay[pl.ds(pl.multiple_of(me * (PAY // 2), PAY // 2), PAY // 2), :] = mine[...]
    pay[pl.ds(pl.multiple_of((1 - me) * (PAY // 2), PAY // 2), PAY // 2), :] = other[...]
    for t in range(14):
        tile = pay[t * 64 : (t + 1) * 64, :]
        turned = pltpu.roll(tile, 64, 1)
        kout[2 * t] = tile[:, :64]
        if t < 13:
            kout[2 * t + 1] = turned[:, :64]
        else:
            bout[...] = turned[0:1, :64]


VM = pl.BlockSpec(memory_space=pltpu.VMEM)
SM = pl.BlockSpec(memory_space=pltpu.SMEM)
ANY = pl.BlockSpec(memory_space=pl.ANY)
ROOM = pltpu.CompilerParams(vmem_limit_bytes=32 * 2**20)


def sds(shape, dtype=F32):
    return jax.ShapeDtypeStruct(shape, dtype)


def both_ways(low, high, ids, axis):
    lines = np.moveaxis(ids, axis, -1)
    steps = [(int(a), int(b)) for a, b in zip(lines[..., :-1].ravel(), lines[..., 1:].ravel())]
    up = lax.ppermute(high, AX, steps)
    down = lax.ppermute(low, AX, [(b, a) for a, b in steps])
    return up, down


def sum_groups(ids):
    zh, x, y, zl, _ = ids.shape
    first, second = [], []
    for core in range(2):
        part = ids[..., core]
        if core == 0 or y != zh * zl:
            first += part.transpose(0, 3, 1, 2).reshape(zh * zl, x * y).tolist()
            second += part.transpose(1, 2, 0, 3).reshape(x * y, zh * zl).tolist()
        else:
            first += part.transpose(2, 1, 0, 3).reshape(y, x * zh * zl).tolist()
            second += part.transpose(1, 0, 3, 2).reshape(x * zh * zl, y).tolist()
    return first, second


def vm(shape, dtype=F32):
    return pltpu.VMEM(shape, dtype)


def local(x):
    return pltpu.with_memory_space_constraint(x, pltpu.VMEM)


def far(x):
    return pltpu.with_memory_space_constraint(x, pltpu.HBM)


def shards(grid, features, preact, cotangent, kernel, active, owner_dir, owner_slot, send_list):
    blocks, channels, volume = features.shape
    listed = send_list.shape[0]
    lay = layout_of(blocks, listed)
    face, yr, zr = lay["face"], lay["y_rows"], lay["z_rows"]
    rows = blocks * VOL
    devices = int(np.prod(grid))
    ids = np.arange(devices).reshape(grid)
    core = (lax.axis_index(AX) & 1).astype(jnp.int32).reshape(1)
    scale = float((volume * blocks * devices) ** -0.5)

    gd, xs0, xs1, ys, zs = pl.pallas_call(
        prep_kernel,
        out_shape=(vm((rows, LANES)), vm((face // 2, LANES)), vm((face // 2, LANES)), vm((2, face, LANES)), vm((2, face, LANES))),
        in_specs=[SM] + [ANY] * 4,
        out_specs=(VM,) * 5,
        scratch_shapes=[
            pltpu.SMEM((listed,), jnp.int32),
            pltpu.VMEM((blocks, channels, VOL), F32),
            pltpu.VMEM((blocks, channels, VOL), F32),
            pltpu.VMEM((blocks, VOL), jnp.int32),
            pltpu.SemaphoreType.DMA((blocks, 2)),
            pltpu.SemaphoreType.DMA,
            pltpu.SemaphoreType.DMA,
            pltpu.VMEM((2, face, LANES), F32),
        ],
        name="prep", compiler_params=ROOM,
    )(core, far(send_list), far(cotangent), far(preact), far(active))
    rx0, rx1 = both_ways(xs0, xs1, ids, 0)

    third = max(blocks // 4, 1)
    parts = (range(third), range(third, 2 * third), range(2 * third, blocks))

    def scratch(part):
        return [
            pltpu.VMEM((VOL, 1152), BF16),
            pltpu.VMEM((max(len(part), 1), channels, VOL), F32),
            pltpu.SemaphoreType.DMA((max(len(part), 1),)),
        ]

    wide = (384, 1152)
    n0 = len(parts[0]) * VOL
    at0, p0, kg, rt, bias = pl.pallas_call(
        functools.partial(first_kernel, parts[0]),
        in_specs=[VM, ANY, VM, ANY],
        out_specs=(VM,) * 5,
        out_shape=(vm((n0, LANES)), vm((n0, LANES)), vm(wide), vm(wide, BF16), vm((8, LANES))),
        scratch_shapes=scratch(parts[0]) + [pltpu.VMEM((27, channels, channels), F32), pltpu.SemaphoreType.DMA],
        name="interior0", compiler_params=ROOM,
    )(local(gd), far(features), active, far(kernel))

    def more(part, earlier, kg, bias, after, name):
        n = len(part) * VOL + sum(e.shape[0] for e in earlier[::2])
        return pl.pallas_call(
            functools.partial(next_kernel, part, len(earlier) // 2),
            in_specs=[VM, ANY] + [VM] * (4 + len(earlier)) + [ANY],
            out_specs=(VM,) * 5,
            out_shape=(vm((n, LANES)), vm((n, LANES)), vm(wide), vm((8, LANES)),
                       vm((16, LANES) if earlier else (4, 128, 1152), BF16)),
            scratch_shapes=scratch(part),
            name=name, compiler_params=ROOM,
        )(local(gd), far(features), active, local(rt), local(kg), local(bias), *[local(e) for e in earlier], after)

    ys0, ys1 = pl.pallas_call(
        pack_y_kernel, out_shape=(vm((yr // 2, LANES)),) * 2,
        scratch_shapes=[pltpu.VMEM((2, face, LANES), F32), pltpu.VMEM((yr, LANES), F32)],
        in_specs=[VM] * 3 + [ANY], out_specs=(VM,) * 2,
        name="pack_y", compiler_params=ROOM,
    )(local(ys), local(rx0), local(rx1), bias)
    ry0, ry1 = both_ways(ys0, ys1, ids, 1)
    at1, p1, kg, bias, rtp = more(parts[1], (), kg, bias, ys0, "interior1")
    zs0, zs1 = pl.pallas_call(
        pack_z_kernel, out_shape=(vm((zr // 2, LANES)),) * 2,
        scratch_shapes=[pltpu.VMEM((n, LANES), F32) for n in (face, face, yr, yr, zr)],
        in_specs=[VM] * 5 + [ANY], out_specs=(VM,) * 2,
        name="pack_z", compiler_params=ROOM,
    )(local(zs), local(rx0), local(rx1), local(ry0), local(ry1), bias)
    rz0, rz1 = both_ways(zs0, zs1, ids, 2)
    at, p, kg, bias, _ = more(parts[2], (at0, p0, at1, p1), kg, bias, zs0, "interior2")

    table = jnp.asarray(piece_table(blocks, listed))
    mine, other, pws = pl.pallas_call(
        functools.partial(halo_kernel, scale),
        out_shape=(vm((PAY // 2, LANES)), vm((PAY // 2, LANES)), vm((6 * blocks, 64, 1152), BF16)),
        in_specs=[SM] * 4 + [VM] * 10,
        out_specs=(VM,) * 3,
        scratch_shapes=[
            pltpu.VMEM((lay["total"], LANES), F32),
            pltpu.VMEM((10, 24, LANES), F32),
            pltpu.VMEM((PAY, LANES), F32),
            pltpu.VMEM((384, 1152), F32),
        ],
        name="halo", compiler_params=ROOM,
    )(owner_dir, owner_slot, table, core, local(gd), local(rx0), local(rx1), local(ry0), local(ry1),
      local(rz0), local(rz1), local(at), local(bias), local(kg))

    swap = [(i, i ^ 1) for i in range(devices)]
    arrived = lax.ppermute(other, AX, swap)
    p = pl.pallas_call(
        edges_kernel, out_shape=vm((rows, LANES)), in_specs=[SM] + [VM] * 4, out_specs=VM,
        name="edges", compiler_params=ROOM,
    )(owner_dir, local(pws), local(rt), local(rtp), local(p))
    half = pl.pallas_call(
        join_kernel, out_shape=vm((PAY // 2, LANES)), in_specs=[VM, VM, ANY], out_specs=VM,
        name="join", compiler_params=ROOM,
    )(local(mine), local(arrived), p)
    over, along = sum_groups(ids.reshape(2, grid[0] // 2, grid[1], grid[2] // 2, 2))
    plane, depth = len(over[0]), len(along[0])
    chunk = PAY // 2 // plane // 2

    def trade(x, groups):
        x = x.reshape(len(groups[0]) * chunk, 2, LANES)
        x = lax.all_to_all(x, AX, 0, 0, tiled=True, axis_index_groups=groups)
        return x.reshape(len(groups[0]), chunk, 2, LANES)

    def copies(x, count):
        return jnp.broadcast_to(x[None], (count,) + x.shape)

    share = jnp.sum(trade(half, over), axis=0)
    share = jnp.sum(trade(copies(share, depth), along), axis=0)
    whole = trade(copies(share, plane), over)
    whole = whole.reshape(PAY // 2, LANES)
    rest = lax.ppermute(whole, AX, swap)
    input_grad = pl.pallas_call(
        finish_kernel, out_shape=sds((blocks, channels, VOL)), in_specs=[VM] * 2, out_specs=VM,
        name="finish", compiler_params=ROOM,
    )(local(p), active)

    kernel_grad, bias_grad = pl.pallas_call(
        unpack_kernel,
        out_shape=(sds((27, channels, channels)), sds((1, channels))),
        in_specs=[SM, VM, VM],
        out_specs=(VM,) * 2,
        scratch_shapes=[pltpu.VMEM((PAY, LANES), F32)],
        name="unpack", compiler_params=ROOM,
    )(core, local(whole), local(rest))
    return input_grad, kernel_grad, bias_grad.reshape(channels)


def solution(mesh):
    grid = mesh.devices.shape
    flat = Mesh(mesh.devices.reshape(-1), (AX,))
    placed = (
        P(AX, None, None),
        P(AX, None, None),
        P(AX, None, None),
        P(),
        P(AX, None),
        P(AX, None),
        P(AX, None),
        P(AX),
    )
    return jax.shard_map(
        functools.partial(shards, grid),
        mesh=flat,
        in_specs=placed,
        out_specs=(P(AX, None, None), P(), P()),
        check_vma=False,
    )
```

```python
import functools

import jax
import jax.numpy as jnp
import numpy as np
from jax import lax
from jax.experimental import pallas as pl
from jax.experimental.pallas import tpu as pltpu
from jax.sharding import Mesh, PartitionSpec as P

F32 = jnp.float32
BF16 = jnp.bfloat16
BS = 8
VOL = 512
LANES = 128
PAY = 896
AX = "d"

FACE = 64


def layout_of(blocks, listed):
    face = listed * FACE
    edge = listed * BS
    corner = -(-listed // 8) * 8
    y_rows = face + 2 * edge
    z_rows = face + 4 * edge + 4 * corner
    starts = [0]
    for size in (face, face, y_rows, y_rows, z_rows):
        starts.append(starts[-1] + size)
    total = starts[-1] + z_rows
    return dict(face=face, edge=edge, corner=corner, y_rows=y_rows, z_rows=z_rows,
                starts=starts, total=total)


def log2(n):
    return int(n).bit_length() - 1


def piece_table(blocks, listed):
    lay = layout_of(blocks, listed)
    face, edge, corner, starts = lay["face"], lay["edge"], lay["corner"], lay["starts"]
    table = np.zeros((27, 28), np.int32)
    for o in range(27):
        off = (o // 9 - 1, o // 3 % 3 - 1, o % 3 - 1)
        if off == (0, 0, 0):
            continue
        fixed = [7 if v == -1 else 0 for v in off]
        axis = 0 if off[0] else (1 if off[1] else 2)
        plane = [i for i in range(3) if i != axis]
        for d in range(27):
            own = (d // 9 - 1, d // 3 % 3 - 1, d % 3 - 1)
            if any(v != 0 and v != w for v, w in zip(own, off)):
                continue
            side = [(v + 1) // 2 for v in own]
            if own == (0, 0, 0):
                base, mult, strides = 0, VOL, {0: 64, 1: 8, 2: 1}
            elif own[2]:
                base = starts[4 + side[2]]
                if own[0] and own[1]:
                    base += face + 4 * edge + corner * (side[1] * 2 + side[0])
                    mult, strides = 1, {}
                elif own[0]:
                    base += face + edge * side[0]
                    mult, strides = 8, {1: 1}
                elif own[1]:
                    base += face + 2 * edge + edge * side[1]
                    mult, strides = 8, {0: 1}
                else:
                    mult, strides = 64, {0: 8, 1: 1}
            elif own[1]:
                base = starts[2 + side[1]]
                if own[0]:
                    base += face + edge * side[0]
                    mult, strides = 8, {2: 1}
                else:
                    mult, strides = 64, {0: 8, 2: 1}
            else:
                base = starts[side[0]]
                mult, strides = 64, {1: 8, 2: 1}
            for i in range(3):
                if off[i] != 0:
                    base += fixed[i] * strides.get(i, 0)
            s1 = strides[plane[0]] if off[plane[0]] == 0 else 1
            s2 = strides[plane[1]] if off[plane[1]] == 0 else 1
            table[o, d] = base | log2(mult) << 12 | log2(s1) << 16 | log2(s2) << 20
    return table.reshape(-1)


def split_hl(value, mask):
    high = value.astype(BF16).astype(F32)
    return jnp.where(mask, high, value - high)


def pack_rows(ref, out):
    n = out.shape[0]
    left = lax.broadcasted_iota(jnp.int32, (n, LANES), 1) < 64
    out[...] = jnp.where(left, ref[0:n, :], ref[n : 2 * n, :])


def unpack_rows(ref, out, start=0):
    n = ref.shape[0]
    left = lax.broadcasted_iota(jnp.int32, (n, LANES), 1) < 64
    v = ref[...]
    w = pltpu.roll(v, 64, 1)
    out[start : start + n, :] = jnp.where(left, v, w)
    out[start + n : start + 2 * n, :] = jnp.where(left, w, v)


def prep_kernel(core, send_h, cot_h, pre_h, act_h, gd, xs0, xs1, ys, zs, send, cot, pre, act, sems, asem, ssem, xf):
    blocks = cot.shape[0]
    listed = send.shape[0]
    pairs = ((cot_h, cot, 0), (pre_h, pre, 1))
    copies = [[pltpu.make_async_copy(h.at[b], v.at[b], sems.at[b, i]) for h, v, i in pairs] for b in range(blocks)]
    act_copy = pltpu.make_async_copy(act_h, act, asem)
    send_copy = pltpu.make_async_copy(send_h, send, ssem)
    act_copy.start()
    for pair in copies:
        for copy in pair:
            copy.start()
    send_copy.start()
    act_copy.wait()
    for b in range(blocks):
        for copy in copies[b]:
            copy.wait()
        p = pre[b]
        s = 1.0 / (1.0 + jnp.exp(-p))
        m = act[b : b + 1, :].astype(F32)
        g = cot[b] * (s * (1.0 + p * (1.0 - s))) * m
        gd[b * VOL : (b + 1) * VOL, :] = jnp.concatenate([g, g], axis=0).T
    send_copy.wait()
    for i in range(listed):
        r0 = pl.multiple_of(jnp.minimum(send[i], blocks - 1) * VOL, VOL)
        for side in range(2):
            f = 7 * side
            xf[side, i * 64 : (i + 1) * 64, :] = gd[pl.ds(r0 + f * 64, 64), :]
            for x in range(8):
                ys[side, i * 64 + x * 8 : i * 64 + x * 8 + 8, :] = gd[pl.ds(r0 + x * 64 + f * 8, 8), :]
            zs[side, i * 64 : (i + 1) * 64, :] = gd[pl.ds(r0 + f, 64, stride=8), :]
    pack_rows(xf.at[0], xs0)
    pack_rows(xf.at[1], xs1)


def pack_y_kernel(ys, rx0, rx1, after, out0, out1, xf, yf):
    face = ys.shape[1]
    listed = face // 64
    unpack_rows(rx0, xf.at[0])
    unpack_rows(rx1, xf.at[1])
    for side, out in ((0, out0), (1, out1)):
        f = 7 * side
        yf[0:face, :] = ys[side]
        for j in range(2):
            for s in range(listed):
                row = face + (j * listed + s) * 8
                yf[row : row + 8, :] = xf[j, s * 64 + f * 8 : s * 64 + f * 8 + 8, :]
        pack_rows(yf, out)


def pack_z_kernel(zs, rx0, rx1, ry0, ry1, after, out0, out1, x0, x1, y0, y1, zf):
    face = zs.shape[1]
    listed = face // 64
    edge = listed * 8
    corner = -(-listed // 8) * 8
    for src, full in ((rx0, x0), (rx1, x1), (ry0, y0), (ry1, y1)):
        unpack_rows(src, full)
    for side, out in ((0, out0), (1, out1)):
        f = 7 * side
        zf[0:face, :] = zs[side]
        for j, src in enumerate((x0, x1, y0, y1)):
            row = face + j * edge
            zf[row : row + edge, :] = src[pl.ds(f, edge, stride=8), :]
        for j, src in enumerate((y0, y1)):
            for i in range(2):
                row = face + 4 * edge + corner * (2 * j + i)
                zf[row : row + corner, :] = jnp.zeros((corner, LANES), F32)
                for s in range(listed):
                    at = face + i * edge + s * 8 + f
                    zf[row + s : row + s + 1, :] = src[at : at + 1, :]
        pack_rows(zf, out)


def interior_block(b, r0, gd, feat, act, at, p, kg_in, kg, rt, bias_in, bias, z):
    lane = lax.broadcasted_iota(jnp.int32, (VOL, LANES), 1) < 64
    rows = slice(r0, r0 + VOL)
    g = gd[b * VOL : (b + 1) * VOL, :]
    total = jnp.broadcast_to(jnp.sum(g, axis=0, keepdims=True), bias.shape)
    bias[...] = total if bias_in is None else bias_in[...] + total
    hl = split_hl(g, lane)
    row = lax.broadcasted_iota(jnp.int32, (VOL, LANES), 0)
    vy = (row // 8) % 8
    vz = row % 8
    for kz in (-1, 0, 1):
        if kz == 0:
            sz = hl
        elif kz == 1:
            sz = jnp.where(vz >= 1, pltpu.roll(hl, 1, 0), 0.0)
        else:
            sz = jnp.where(vz <= 6, pltpu.roll(hl, VOL - 1, 0), 0.0)
        for ky in (-1, 0, 1):
            if ky == 0:
                sy = sz
            elif ky == 1:
                sy = jnp.where(vy >= 1, pltpu.roll(sz, 8, 0), 0.0)
            else:
                sy = jnp.where(vy <= 6, pltpu.roll(sz, VOL - 8, 0), 0.0)
            c = (ky + 1) * 3 + kz + 1
            z[:, c * 128 : (c + 1) * 128] = sy.astype(BF16)

    f = feat * act[b : b + 1, :].astype(F32)
    ff = jnp.concatenate([f, f], axis=0)
    half = lax.broadcasted_iota(jnp.int32, (LANES, VOL), 0) < 64
    a = split_hl(ff, half)
    at[rows, :] = a.T
    zero = jnp.zeros((LANES, 64), F32)
    up = jnp.concatenate([zero, a[:, : VOL - 64]], axis=1)
    down = jnp.concatenate([a[:, 64:], zero], axis=1)
    a3 = jnp.concatenate([up, a, down], axis=0).astype(BF16)
    term = jnp.dot(a3, z[...], preferred_element_type=F32)
    kg[...] = term if kg_in is None else kg_in[...] + term
    p3 = lax.dot_general(z[...], rt[...], (((1,), (1,)), ((), ())), preferred_element_type=F32)
    p[rows, :] = p3[:, 128:256]
    p[r0 + 64 : r0 + VOL, :] += p3[: VOL - 64, 256:384]
    p[r0 : r0 + VOL - 64, :] += p3[64:, 0:128]


def fetch(part, feat_h, feat, sems):
    return [pltpu.make_async_copy(feat_h.at[b], feat.at[i], sems.at[i]) for i, b in enumerate(part)]


def first_kernel(part, gd, feat_h, act, kern_h, at, p, kg, rt, bias, z, feat, sems, kern, ksem):
    kern_copy = pltpu.make_async_copy(kern_h, kern, ksem)
    kern_copy.start()
    copies = fetch(part, feat_h, feat, sems)
    for copy in copies:
        copy.start()
    kern_copy.wait()
    for k in range(27):
        kx, c = k // 9, k % 9
        w = kern[k]
        wd = jnp.concatenate([w, w], axis=1)
        high = wd.astype(BF16)
        low = (wd - high.astype(F32)).astype(BF16)
        rt[kx * 128 : kx * 128 + 64, c * 128 : (c + 1) * 128] = high
        rt[kx * 128 + 64 : kx * 128 + 128, c * 128 : (c + 1) * 128] = low
    for i, b in enumerate(part):
        copies[i].wait()
        kgi, bi = (None, None) if i == 0 else (kg, bias)
        interior_block(b, i * VOL, gd, feat[i], act, at, p, kgi, kg, rt, bi, bias, z)


def plane_weights(rt, rtp):
    for i in range(3):
        rows = slice(i * 128, (i + 1) * 128)
        for s, k in enumerate((0, 2)):
            rtp[s, :, i * 384 : (i + 1) * 384] = rt[rows, k * 384 : (k + 1) * 384]
            for j in range(3):
                c = i * 3 + j
                rtp[2 + s, :, c * 128 : (c + 1) * 128] = rt[rows, (j * 3 + k) * 128 : (j * 3 + k + 1) * 128]


def next_kernel(part, held, *refs):
    gd, feat_h, act, rt, kg0, bias0 = refs[:6]
    earlier = refs[6 : 6 + 2 * held]
    at, p, kg, bias, rtp, z, feat, sems = refs[7 + 2 * held :]
    copies = fetch(part, feat_h, feat, sems)
    for copy in copies:
        copy.start()
    if held:
        rtp[...] = jnp.zeros(rtp.shape, rtp.dtype)
    else:
        plane_weights(rt, rtp)
    row = 0
    for i in range(held):
        n = earlier[2 * i].shape[0]
        at[row : row + n, :] = earlier[2 * i][...]
        p[row : row + n, :] = earlier[2 * i + 1][...]
        row += n
    for i, b in enumerate(part):
        copies[i].wait()
        kgi, bi = (kg0, bias0) if i == 0 else (kg, bias)
        interior_block(b, row + i * VOL, gd, feat[i], act, at, p, kgi, kg, rt, bi, bias, z)


def nt(a, b):
    return lax.dot_general(a, b, (((1,), (1,)), ((), ())), preferred_element_type=F32)


def tn(a, b):
    return lax.dot_general(a, b, (((0,), (0,)), ((), ())), preferred_element_type=F32)


def plane_pieces(axis, sign):
    out = []
    for o in range(27):
        off = (o // 9 - 1, o // 3 % 3 - 1, o % 3 - 1)
        if off[axis] == sign and all(off[i] == 0 for i in range(axis)):
            r, q = [off[i] for i in range(3) if i != axis]
            out.append((o, r, q))
    return out


def plane_slot(b, axis, sign):
    return b * 6 + 2 * axis + (sign + 1) // 2


def for_planes(od, visit):
    def block(b, carry):
        for axis in range(3):
            for sign in (-1, 1):
                pieces = plane_pieces(axis, sign)
                found = od[b, pieces[0][0]] != 27
                for o, _, _ in pieces[1:]:
                    found = found | (od[b, o] != 27)

                @pl.when(found)
                def _(axis=axis, sign=sign):
                    visit(b, axis, sign)

        return carry

    lax.fori_loop(0, od.shape[0], block, 0)


def edges_kernel(od, pws, rt, rtp, p, pa):
    pa[...] = p[...]

    def plane(b, axis, sign):
        face = 0 if sign == -1 else 7
        pw = pws[plane_slot(b, axis, sign)]
        r0 = b * VOL
        k = 1 - sign
        if axis == 0:
            rows = pl.ds(pl.multiple_of(r0 + face * 64, 64), 64)
            pa[rows, :] += nt(pw, rt[k * 128 : (k + 1) * 128, :])
        elif axis == 1:
            acc = nt(pw, rtp[k // 2])
            for x in range(8):
                rows = pl.ds(pl.multiple_of(r0 + x * 64 + face * 8, 8), 8)
                pa[rows, :] += acc[x * 8 : x * 8 + 8, :]
        else:
            rows = pl.ds(r0 + face, 64, stride=8)
            pa[rows, :] = pa[rows, :] + nt(pw, rtp[2 + k // 2])

    for_planes(od, plane)


def join_kernel(mine, arrived, after, half):
    half[...] = mine[...] + arrived[...]


def halo_kernel(scale, od, os_, tb, core, gd, rx0, rx1, ry0, ry1, rz0, rz1, at, bias, kg0,
                mine, other, pws, src, pb, pay, kg):
    blocks = od.shape[0]
    row = 0
    for ref in (rx0, rx1, ry0, ry1, rz0, rz1):
        unpack_rows(ref, src, row)
        row += 2 * ref.shape[0]
    kg[...] = kg0[...]
    lane64 = lax.broadcasted_iota(jnp.int32, (64, LANES), 1) < 64
    lane24 = lax.broadcasted_iota(jnp.int32, (10, 24, LANES), 2) < 64

    def plane(b, axis, sign):
        face = 0 if sign == -1 else 7
        pw = pws.at[plane_slot(b, axis, sign)]
        pb[...] = jnp.zeros(pb.shape, F32)
        for o, r, q in plane_pieces(axis, sign):
            d = od[b, o]

            @pl.when(d != 27)
            def _(o=o, r=r, q=q, d=d):
                code = tb[o * 28 + d]
                base = (code & 4095) + (os_[b, o] << ((code >> 12) & 15))
                sr = (code >> 16) & 15
                sq = (code >> 20) & 15

                def fill(ref, own):
                    if r == 0 and q == 0:
                        for i in range(8):
                            start = base + (i << sr)
                            if axis == 2 and own:
                                rows = pl.ds(start, 8, stride=8)
                            else:
                                rows = pl.ds(pl.multiple_of(start, 8), 8)
                            pb[i + 1, 8:16, :] = ref[rows, :]
                        return
                    for i in range(8 if r == 0 else 1):
                        for j in range(8 if q == 0 else 1):
                            at_r = i + 1 if r == 0 else (0 if r == -1 else 9)
                            at_q = 8 + j if q == 0 else (7 if q == -1 else 16)
                            row = base + (i << sr) + (j << sq)
                            pb[at_r, at_q : at_q + 1, :] = ref[pl.ds(row, 1), :]

                pl.when(d == 13)(lambda: fill(gd, True))
                pl.when(d != 13)(lambda: fill(src, False))

        pb[...] = split_hl(pb[...], lane24)
        for kr in (-1, 0, 1):
            for kq in (-1, 0, 1):
                win = pb[1 - kr : 9 - kr, 8 - kq : 16 - kq, :].reshape(64, LANES)
                c = (kr + 1) * 3 + kq + 1
                pw[:, c * 128 : (c + 1) * 128] = win.astype(BF16)
        r0 = b * VOL
        k = 1 - sign
        if axis == 0:
            ap = at[pl.ds(pl.multiple_of(r0 + face * 64, 64), 64), :]
        elif axis == 1:
            starts = [pl.multiple_of(r0 + x * 64 + face * 8, 8) for x in range(8)]
            ap = jnp.concatenate([at[pl.ds(s, 8), :] for s in starts], axis=0)
        else:
            ap = at[pl.ds(r0 + face, 64, stride=8), :]
        term = tn(ap.astype(BF16), pw[...])
        if axis == 0:
            kg[k * 128 : (k + 1) * 128, :] += term
        elif axis == 1:
            for i in range(3):
                kg[i * 128 : (i + 1) * 128, k * 384 : (k + 1) * 384] += term[:, i * 384 : (i + 1) * 384]
        else:
            for i in range(3):
                for j in range(3):
                    c = i * 3 + j
                    kg[i * 128 : (i + 1) * 128, (j * 3 + k) * 128 : (j * 3 + k + 1) * 128] += (
                        term[:, c * 128 : (c + 1) * 128]
                    )

    for_planes(od, plane)

    for n in range(28):
        t, odd = n // 2, n % 2
        if n < 27:
            kx, c = n // 9, n % 9
            lo, hi = c * 128, (c + 1) * 128
            u = kg[kx * 128 : kx * 128 + 64, lo:hi] + kg[kx * 128 + 64 : kx * 128 + 128, lo:hi]
            u = u + pltpu.roll(u, 64, 1)
        else:
            first = lax.broadcasted_iota(jnp.int32, (64, LANES), 0) == 0
            u = jnp.where(first, jnp.broadcast_to(bias[0:1, :], (64, LANES)), 0.0)
        if odd:
            pay[t * 64 : (t + 1) * 64, :] = jnp.where(lane64, held, u) * scale
        held = u
    me = core[0]
    mine[...] = pay[pl.ds(pl.multiple_of(me * (PAY // 2), PAY // 2), PAY // 2), :]
    other[...] = pay[pl.ds(pl.multiple_of((1 - me) * (PAY // 2), PAY // 2), PAY // 2), :]


def finish_kernel(pa, act, ig):
    for b in range(act.shape[0]):
        og = pa[b * VOL : (b + 1) * VOL, :]
        og = (og + pltpu.roll(og, 64, 1)).T
        ig[b] = og[:64, :] * act[b : b + 1, :].astype(F32)


def unpack_kernel(core, mine, other, kout, bout, pay):
    me = core[0]
    pay[pl.ds(pl.multiple_of(me * (PAY // 2), PAY // 2), PAY // 2), :] = mine[...]
    pay[pl.ds(pl.multiple_of((1 - me) * (PAY // 2), PAY // 2), PAY // 2), :] = other[...]
    for t in range(14):
        tile = pay[t * 64 : (t + 1) * 64, :]
        turned = pltpu.roll(tile, 64, 1)
        kout[2 * t] = tile[:, :64]
        if t < 13:
            kout[2 * t + 1] = turned[:, :64]
        else:
            bout[...] = turned[0:1, :64]


VM = pl.BlockSpec(memory_space=pltpu.VMEM)
SM = pl.BlockSpec(memory_space=pltpu.SMEM)
ANY = pl.BlockSpec(memory_space=pl.ANY)
ROOM = pltpu.CompilerParams(vmem_limit_bytes=32 * 2**20)


def sds(shape, dtype=F32):
    return jax.ShapeDtypeStruct(shape, dtype)


def both_ways(low, high, ids, axis):
    lines = np.moveaxis(ids, axis, -1)
    steps = [(int(a), int(b)) for a, b in zip(lines[..., :-1].ravel(), lines[..., 1:].ravel())]
    up = lax.ppermute(high, AX, steps)
    down = lax.ppermute(low, AX, [(b, a) for a, b in steps])
    return up, down


def sum_groups(ids):
    zh, x, y, zl, _ = ids.shape
    first, second = [], []
    for core in range(2):
        part = ids[..., core]
        if core == 1 or y != zh * zl:
            first += part.transpose(0, 3, 1, 2).reshape(zh * zl, x * y).tolist()
            second += part.transpose(1, 2, 0, 3).reshape(x * y, zh * zl).tolist()
        else:
            first += part.transpose(2, 1, 0, 3).reshape(y, x * zh * zl).tolist()
            second += part.transpose(1, 0, 3, 2).reshape(x * zh * zl, y).tolist()
    return first, second


def vm(shape, dtype=F32):
    return pltpu.VMEM(shape, dtype)


def local(x):
    return pltpu.with_memory_space_constraint(x, pltpu.VMEM)


def far(x):
    return pltpu.with_memory_space_constraint(x, pltpu.HBM)


def shards(grid, features, preact, cotangent, kernel, active, owner_dir, owner_slot, send_list):
    blocks, channels, volume = features.shape
    listed = send_list.shape[0]
    lay = layout_of(blocks, listed)
    face, yr, zr = lay["face"], lay["y_rows"], lay["z_rows"]
    rows = blocks * VOL
    devices = int(np.prod(grid))
    ids = np.arange(devices).reshape(grid)
    core = (lax.axis_index(AX) & 1).astype(jnp.int32).reshape(1)
    scale = float((volume * blocks * devices) ** -0.5)

    gd, xs0, xs1, ys, zs = pl.pallas_call(
        prep_kernel,
        out_shape=(vm((rows, LANES)), vm((face // 2, LANES)), vm((face // 2, LANES)), vm((2, face, LANES)), vm((2, face, LANES))),
        in_specs=[SM] + [ANY] * 4,
        out_specs=(VM,) * 5,
        scratch_shapes=[
            pltpu.SMEM((listed,), jnp.int32),
            pltpu.VMEM((blocks, channels, VOL), F32),
            pltpu.VMEM((blocks, channels, VOL), F32),
            pltpu.VMEM((blocks, VOL), jnp.int32),
            pltpu.SemaphoreType.DMA((blocks, 2)),
            pltpu.SemaphoreType.DMA,
            pltpu.SemaphoreType.DMA,
            pltpu.VMEM((2, face, LANES), F32),
        ],
        name="prep", compiler_params=ROOM,
    )(core, far(send_list), far(cotangent), far(preact), far(active))
    rx0, rx1 = both_ways(xs0, xs1, ids, 0)

    third = max(blocks // 4, 1)
    parts = (range(third), range(third, 2 * third), range(2 * third, blocks))

    def scratch(part):
        return [
            pltpu.VMEM((VOL, 1152), BF16),
            pltpu.VMEM((max(len(part), 1), channels, VOL), F32),
            pltpu.SemaphoreType.DMA((max(len(part), 1),)),
        ]

    wide = (384, 1152)
    n0 = len(parts[0]) * VOL
    at0, p0, kg, rt, bias = pl.pallas_call(
        functools.partial(first_kernel, parts[0]),
        in_specs=[VM, ANY, VM, ANY],
        out_specs=(VM,) * 5,
        out_shape=(vm((n0, LANES)), vm((n0, LANES)), vm(wide), vm(wide, BF16), vm((8, LANES))),
        scratch_shapes=scratch(parts[0]) + [pltpu.VMEM((27, channels, channels), F32), pltpu.SemaphoreType.DMA],
        name="interior0", compiler_params=ROOM,
    )(local(gd), far(features), active, far(kernel))

    def more(part, earlier, kg, bias, after, name):
        n = len(part) * VOL + sum(e.shape[0] for e in earlier[::2])
        return pl.pallas_call(
            functools.partial(next_kernel, part, len(earlier) // 2),
            in_specs=[VM, ANY] + [VM] * (4 + len(earlier)) + [ANY],
            out_specs=(VM,) * 5,
            out_shape=(vm((n, LANES)), vm((n, LANES)), vm(wide), vm((8, LANES)),
                       vm((16, LANES) if earlier else (4, 128, 1152), BF16)),
            scratch_shapes=scratch(part),
            name=name, compiler_params=ROOM,
        )(local(gd), far(features), active, local(rt), local(kg), local(bias), *[local(e) for e in earlier], after)

    ys0, ys1 = pl.pallas_call(
        pack_y_kernel, out_shape=(vm((yr // 2, LANES)),) * 2,
        scratch_shapes=[pltpu.VMEM((2, face, LANES), F32), pltpu.VMEM((yr, LANES), F32)],
        in_specs=[VM] * 3 + [ANY], out_specs=(VM,) * 2,
        name="pack_y", compiler_params=ROOM,
    )(local(ys), local(rx0), local(rx1), bias)
    ry0, ry1 = both_ways(ys0, ys1, ids, 1)
    at1, p1, kg, bias, rtp = more(parts[1], (), kg, bias, ys0, "interior1")
    zs0, zs1 = pl.pallas_call(
        pack_z_kernel, out_shape=(vm((zr // 2, LANES)),) * 2,
        scratch_shapes=[pltpu.VMEM((n, LANES), F32) for n in (face, face, yr, yr, zr)],
        in_specs=[VM] * 5 + [ANY], out_specs=(VM,) * 2,
        name="pack_z", compiler_params=ROOM,
    )(local(zs), local(rx0), local(rx1), local(ry0), local(ry1), bias)
    rz0, rz1 = both_ways(zs0, zs1, ids, 2)
    at, p, kg, bias, _ = more(parts[2], (at0, p0, at1, p1), kg, bias, zs0, "interior2")

    table = jnp.asarray(piece_table(blocks, listed))
    mine, other, pws = pl.pallas_call(
        functools.partial(halo_kernel, scale),
        out_shape=(vm((PAY // 2, LANES)), vm((PAY // 2, LANES)), vm((6 * blocks, 64, 1152), BF16)),
        in_specs=[SM] * 4 + [VM] * 10,
        out_specs=(VM,) * 3,
        scratch_shapes=[
            pltpu.VMEM((lay["total"], LANES), F32),
            pltpu.VMEM((10, 24, LANES), F32),
            pltpu.VMEM((PAY, LANES), F32),
            pltpu.VMEM((384, 1152), F32),
        ],
        name="halo", compiler_params=ROOM,
    )(owner_dir, owner_slot, table, core, local(gd), local(rx0), local(rx1), local(ry0), local(ry1),
      local(rz0), local(rz1), local(at), local(bias), local(kg))

    swap = [(i, i ^ 1) for i in range(devices)]
    arrived = lax.ppermute(other, AX, swap)
    p = pl.pallas_call(
        edges_kernel, out_shape=vm((rows, LANES)), in_specs=[SM] + [VM] * 4, out_specs=VM,
        name="edges", compiler_params=ROOM,
    )(owner_dir, local(pws), local(rt), local(rtp), local(p))
    half = pl.pallas_call(
        join_kernel, out_shape=vm((PAY // 2, LANES)), in_specs=[VM, VM, ANY], out_specs=VM,
        name="join", compiler_params=ROOM,
    )(local(mine), local(arrived), p)
    over, along = sum_groups(ids.reshape(2, grid[0] // 2, grid[1], grid[2] // 2, 2))
    plane, depth = len(over[0]), len(along[0])
    chunk = PAY // 2 // plane // 2

    def trade(x, groups):
        x = x.reshape(len(groups[0]) * chunk, 2, LANES)
        x = lax.all_to_all(x, AX, 0, 0, tiled=True, axis_index_groups=groups)
        return x.reshape(len(groups[0]), chunk, 2, LANES)

    def copies(x, count):
        return jnp.broadcast_to(x[None], (count,) + x.shape)

    share = jnp.sum(trade(half, over), axis=0)
    share = jnp.sum(trade(copies(share, depth), along), axis=0)
    whole = trade(copies(share, plane), over)
    whole = whole.reshape(PAY // 2, LANES)
    rest = lax.ppermute(whole, AX, swap)
    input_grad = pl.pallas_call(
        finish_kernel, out_shape=sds((blocks, channels, VOL)), in_specs=[VM] * 2, out_specs=VM,
        name="finish", compiler_params=ROOM,
    )(local(p), active)

    kernel_grad, bias_grad = pl.pallas_call(
        unpack_kernel,
        out_shape=(sds((27, channels, channels)), sds((1, channels))),
        in_specs=[SM, VM, VM],
        out_specs=(VM,) * 2,
        scratch_shapes=[pltpu.VMEM((PAY, LANES), F32)],
        name="unpack", compiler_params=ROOM,
    )(core, local(whole), local(rest))
    return input_grad, kernel_grad, bias_grad.reshape(channels)


def solution(mesh):
    grid = mesh.devices.shape
    flat = Mesh(mesh.devices.reshape(-1), (AX,))
    placed = (
        P(AX, None, None),
        P(AX, None, None),
        P(AX, None, None),
        P(),
        P(AX, None),
        P(AX, None),
        P(AX, None),
        P(AX),
    )
    return jax.shard_map(
        functools.partial(shards, grid),
        mesh=flat,
        in_specs=placed,
        out_specs=(P(AX, None, None), P(), P()),
        check_vma=False,
    )
```
